32 devices in a mesh: groups: 2 (over y), seq: 4 (over z), batch: 2 (over x), sub: 2 (over core).
Axes of the slice: x: 2, y: 2, z: 4, core: 2. Of those that a mesh axis runs over, the one named last changes fastest.
Arguments:
- gen_hidden: bfloat16 [4, 256, 8192], P(('groups', 'batch'), None, ('seq', 'sub')), parts along dimension 0, may hold values from -6 to 6
- out_proj: bfloat16 [8192, 4096], P(('seq', 'sub')), may hold values from -0.0625 to 0.0625
- norm_gain: bfloat16 [4096], replicated, may hold values from 0.099609375 to 1.8984375
- q_weight: bfloat16 [4096, 4096], P(None, ('seq', 'sub')), may hold values from -0.09375 to 0.09375
- kv_weight: bfloat16 [2, 4096, 1024], P(None, None, ('seq', 'sub')), may hold values from -0.09375 to 0.09375
- kv_cache: bfloat16 [2, 4, 8192, 1024], P(None, ('groups', 'batch'), ('seq', 'sub')), parts along dimension 1, may hold values from -96 to 96
- lengths: int32 [4], P(('groups', 'batch')), parts along dimension 0, may hold values from 1024 to 8192, as said below
- span_start: int32 [4], P(('groups', 'batch')), parts along dimension 0, may hold values from 1024 to 16383, as said below
Outputs:
- attention: bfloat16 [4, 256, 4096], P(('groups', 'batch'), ('seq', 'sub')), parts along dimension 0
The draws below stay inside these ranges and needn't reach their ends.
There are 2 independent parts, one for each index of `groups`. The reference program is written for one: setup_inputs(seed, part) draws one part's arguments, and reference() takes and returns one part's arrays. A program takes and returns all parts, laid end to end along the dimension named above; an argument that names none is the same for every part. Nothing has to cross between parts.
Inputs may be any that keep to these rules, and one draw needn't show every extreme that they name: `lengths`: slots at or past a session's length are not attended. In every draw some session has the full 8192 slots. `span_start`: A session's span starts at or after its window length and less than 8192 later.
All inputs are finite; a program needn't handle non-finite values.
Results may differ from the reference program's by a relative error of at most 0.04.
Values may be sent and summed in bfloat16 or wider, within the bound.
A program may use at most 128 MiB of HBM per device.

```python
import math
import jax
import jax.numpy as jnp
from jax import lax

D_GEN = 8192
D = 4096
QH = 32
KVH = 8
HD = 128
C = 256
WIN = 8192
SESS = 2


def window_draws(key):
    length_key = jax.random.fold_in(key, 101)
    order_key = jax.random.fold_in(key, 202)
    offset_key = jax.random.fold_in(key, 303)
    lengths = jax.random.randint(length_key, (SESS,), WIN // 8, WIN + 1)
    fullest = jax.random.randint(order_key, (), 0, SESS)
    offsets = jax.random.randint(offset_key, (SESS,), 0, WIN)
    picked = jnp.arange(SESS) == fullest
    lengths = jnp.where(picked, WIN, lengths)
    offsets = jnp.where(picked, WIN - 1, offsets)
    starts = lengths + offsets
    return (lengths.astype(jnp.int32), starts.astype(jnp.int32))


def draw_lengths(key, part):
    return window_draws(key)[0]


def draw_span_start(key, part):
    return window_draws(key)[1]


def draw_kv_cache(key, part):
    shape = (2, SESS, WIN, KVH * HD)
    values = jnp.clip(jax.random.normal(jax.random.fold_in(key, 1), shape, jnp.float32), -6.0, 6.0)
    return values.astype(jnp.bfloat16)


def with_spikes(entries, rng, source, target, shards_of, factor):
    def block_of(axis_at):
        return (jnp.arange(entries.shape[axis_at]) // (entries.shape[axis_at] // shards_of)).reshape((-1,) + (1,) * (entries.ndim - 1 - axis_at))

    near = jax.random.permutation(rng, shards_of)[block_of(target)]
    far = (block_of(target) + shards_of // 2) % shards_of
    return jnp.where((block_of(source) == near) | (block_of(source) == far), factor * entries, entries)


def levels(own_key, dims, cuts, smallest, high):
    def one(dim, parts):
        steps = jax.random.uniform(jax.random.fold_in(jax.random.fold_in(own_key, 6), dim), (parts,), jnp.float32, smallest / len(cuts), high / len(cuts))
        return jnp.repeat(jnp.exp(steps), dims[dim] // parts).reshape((-1,) + (1,) * (len(dims) - dim - 1))

    gain = one(*cuts[0])
    for cut in cuts[1:]:
        gain = gain * one(*cut)
    return gain


def gaussian(stream_key, extent, scale, limit, pieces=(), kind=jnp.bfloat16):
    array = scale * jax.random.normal(stream_key, extent, jnp.float32)
    if pieces:
        array = array * levels(stream_key, extent, pieces, -0.22, 0.18)
    return jnp.clip(array, -limit, limit).astype(kind)


def noise_with(key, shape, deviation, bound, shards, heavy, held_as=jnp.bfloat16):
    values = deviation * jax.random.normal(key, shape, jnp.float32)
    if shards:
        values = values * levels(key, shape, shards, -0.22, 0.18)
    return jnp.clip(with_spikes(values, jax.random.fold_in(key, 3), *heavy), -bound, bound).astype(held_as)


def setup_inputs(seed: int = 0, part: int = 0) -> dict:
    streams_of = jax.random.split(jax.random.key(seed), 9)
    own_keys = jax.random.split(jax.random.fold_in(streams_of[8], part), 9)
    gen_hidden = noise_with(own_keys[0], (SESS, C, D_GEN), 1.0, 6.0, ((0, 2), (2, 8)), (2, 1, 8, 2.0))
    out_proj = gaussian(streams_of[1], (D_GEN, D), D_GEN ** -0.5, 0.0625, ((0, 8),))
    norm_gain = jnp.clip(1.0 + 0.18 * jax.random.normal(streams_of[2], (D,), jnp.float32), 0.099609375, 1.8984375).astype(jnp.bfloat16)
    q_weight = gaussian(streams_of[3], (D, QH * HD), D ** -0.5, 0.09375, ((1, 8),))
    kv_weight = gaussian(streams_of[4], (2, D, KVH * HD), D ** -0.5, 0.09375, ((2, 8),))
    kv_cache = draw_kv_cache(jax.random.fold_in(jax.random.fold_in(streams_of[8], part), 71), part)
    lengths = draw_lengths(jax.random.fold_in(jax.random.fold_in(streams_of[8], part), 71), part)
    span_start = draw_span_start(jax.random.fold_in(jax.random.fold_in(streams_of[8], part), 71), part)
    return {"gen_hidden": gen_hidden, "out_proj": out_proj, "norm_gain": norm_gain, "q_weight": q_weight, "kv_weight": kv_weight, "kv_cache": kv_cache, "lengths": lengths, "span_start": span_start}


EPS = 1e-05
THETA = 500000.0
NEG = -1e+30

def rotate(values, positions):
    half = values.shape[-1] // 2
    freq = THETA ** (-jnp.arange(half, dtype=jnp.float32) * 2.0 / values.shape[-1])
    angle = positions.astype(jnp.float32)[..., None] * freq
    cosine = jnp.cos(angle)[..., None, :]
    sine = jnp.sin(angle)[..., None, :]
    first = values[..., :half]
    second = values[..., half:]
    return jnp.concatenate([first * cosine - second * sine, second * cosine + first * sine], axis=-1)

def reference(gen_hidden, out_proj, norm_gain, q_weight, kv_weight, kv_cache, lengths, span_start):
    group = QH // KVH
    scale = 1.0 / math.sqrt(HD)

    def one_session(items):
        hidden, cache_keys, cache_values, length, start = items
        inputs = jnp.dot(hidden, out_proj, preferred_element_type=jnp.float32).astype(jnp.bfloat16)
        wide = inputs.astype(jnp.float32)
        inverse = lax.rsqrt(lax.optimization_barrier(jnp.mean(wide * wide, axis=-1, keepdims=True)) + EPS)
        normed = (wide * inverse * norm_gain.astype(jnp.float32)).astype(jnp.bfloat16)
        positions = start + jnp.arange(C, dtype=jnp.int32)
        query = jnp.dot(normed, q_weight, preferred_element_type=jnp.float32).reshape(C, QH, HD)
        query = rotate(query, positions).astype(jnp.bfloat16)
        key_raw = jnp.dot(normed, kv_weight[0], preferred_element_type=jnp.float32).astype(jnp.bfloat16)
        key_raw = lax.optimization_barrier(key_raw)
        new_keys = rotate(key_raw.astype(jnp.float32).reshape(C, KVH, HD), positions).astype(jnp.bfloat16)
        new_values = jnp.dot(normed, kv_weight[1], preferred_element_type=jnp.float32).astype(jnp.bfloat16)
        keys = jnp.concatenate([cache_keys.reshape(WIN, KVH, HD), new_keys], axis=0).astype(jnp.float32)
        values = jnp.concatenate([cache_values.reshape(WIN, KVH, HD), new_values.reshape(C, KVH, HD)], axis=0).astype(jnp.float32)
        grouped = query.reshape(C, KVH, group, HD).astype(jnp.float32)
        scores = jnp.einsum('cagh,wah->agcw', grouped, keys) * scale
        live_cache = jnp.broadcast_to(jnp.arange(WIN, dtype=jnp.int32)[None, :] < length, (C, WIN))
        causal = jnp.arange(C, dtype=jnp.int32)[None, :] <= jnp.arange(C, dtype=jnp.int32)[:, None]
        live = jnp.concatenate([live_cache, causal], axis=1)
        scores = jnp.where(live, scores, NEG)
        top = lax.optimization_barrier(jnp.max(scores, axis=-1, keepdims=True))
        weights = jnp.exp(scores - top)
        total = lax.optimization_barrier(jnp.sum(weights, axis=-1))
        probs = lax.optimization_barrier(weights.astype(jnp.bfloat16))
        mixed = jnp.einsum('agcw,wah->cagh', probs.astype(jnp.float32), values)
        result = mixed / jnp.transpose(total, (2, 0, 1))[..., None]
        return result.astype(jnp.bfloat16).reshape(C, QH * HD)
    return lax.map(one_session, (gen_hidden, kv_cache[0], kv_cache[1], lengths, span_start))
```

```python
import functools
import math

import jax
import jax.numpy as jnp
from jax import lax
from jax.experimental import pallas as pl
from jax.experimental.pallas import tpu as pltpu
from jax.sharding import PartitionSpec as P

QH = 32
KVH = 8
HD = 128


EPS = 1e-05
THETA = 500000.0
NEG = -1e30


def rotate(values, positions):
    half = values.shape[-1] // 2
    freq = THETA ** (-jnp.arange(half, dtype=jnp.float32) * 2.0 / values.shape[-1])
    angle = positions.astype(jnp.float32)[..., None] * freq
    cosine = jnp.cos(angle)[..., None, :]
    sine = jnp.sin(angle)[..., None, :]
    first = values[..., :half]
    second = values[..., half:]
    return jnp.concatenate(
        [first * cosine - second * sine, second * cosine + first * sine], axis=-1
    )


def body(gen_hidden, out_proj, norm_gain, q_weight, kv_weight, kv_cache, lengths, span_start):
    sessions, span, _ = gen_hidden.shape
    shards = lax.axis_size(("seq", "sub"))
    mine = lax.axis_index(("seq", "sub"))
    rows = span // shards
    local_heads = q_weight.shape[1] // HD
    group = QH // KVH
    scale = 1.0 / math.sqrt(HD)
    window_local = kv_cache.shape[2]
    summed = lax.psum(
        jnp.einsum("sci,id->csd", gen_hidden, out_proj, preferred_element_type=jnp.float32),
        ("seq", "sub"),
    )
    inputs = summed.astype(jnp.bfloat16)
    wide = inputs.astype(jnp.float32)
    inverse = lax.rsqrt(jnp.mean(wide * wide, axis=-1, keepdims=True) + EPS)
    normed = (wide * inverse * norm_gain.astype(jnp.float32)).astype(jnp.bfloat16)
    positions = span_start[None, :] + jnp.arange(span, dtype=jnp.int32)[:, None]
    query = jnp.einsum("csd,dh->csh", normed, q_weight, preferred_element_type=jnp.float32)
    query = rotate(query.reshape(span, sessions, local_heads, HD), positions).astype(jnp.bfloat16)
    kv_raw = jnp.einsum(
        "csd,jdk->jcsk", normed, kv_weight, preferred_element_type=jnp.float32
    ).astype(jnp.bfloat16)
    query_rows = jnp.arange(span, dtype=jnp.int32)
    new_rows = lax.all_to_all(kv_raw, ("seq", "sub"), split_axis=1, concat_axis=3, tiled=True)
    my_positions = lax.dynamic_slice_in_dim(positions, mine * rows, rows, 0)
    new_keys = rotate(
        new_rows[0].reshape(rows, sessions, KVH, HD).astype(jnp.float32), my_positions
    ).astype(jnp.bfloat16)
    new_values = new_rows[1].reshape(rows, sessions, KVH, HD)
    every_query = lax.all_gather(
        query.reshape(span, sessions, local_heads * HD), ("seq", "sub"), axis=2, tiled=True
    )
    grouped = every_query.reshape(span, sessions, KVH, group, HD)
    cached = kv_cache.reshape(2, sessions, window_local, KVH, HD)
    cache_scores = (
        jnp.einsum("csagh,swah->sagcw", grouped, cached[0], preferred_element_type=jnp.float32)
        * scale
    )
    slots = mine * window_local + jnp.arange(window_local, dtype=jnp.int32)
    live = slots[None, :] < lengths[:, None]
    cache_scores = jnp.where(live[:, None, None, None, :], cache_scores, NEG)
    span_scores = (
        jnp.einsum("csagh,tsah->sagct", grouped, new_keys, preferred_element_type=jnp.float32)
        * scale
    )
    key_rows = mine * rows + jnp.arange(rows, dtype=jnp.int32)
    causal = key_rows[None, :] <= query_rows[:, None]
    span_scores = jnp.where(causal, span_scores, NEG)
    top = jnp.maximum(jnp.max(cache_scores, axis=-1), jnp.max(span_scores, axis=-1))
    cache_weights = jnp.exp(cache_scores - top[..., None])
    span_weights = jnp.exp(span_scores - top[..., None])
    total = jnp.sum(cache_weights, axis=-1) + jnp.sum(span_weights, axis=-1)
    mixed = jnp.einsum(
        "sagcw,swah->scagh",
        cache_weights.astype(jnp.bfloat16),
        cached[1],
        preferred_element_type=jnp.float32,
    )
    mixed = mixed + jnp.einsum(
        "sagct,tsah->scagh",
        span_weights.astype(jnp.bfloat16),
        new_values,
        preferred_element_type=jnp.float32,
    )
    partial_value = mixed.reshape(1, sessions, span, QH * HD)
    peak = jnp.transpose(top, (0, 3, 1, 2)).reshape(1, sessions, span, QH)
    mass = jnp.transpose(total, (0, 3, 1, 2)).reshape(1, sessions, span, QH)
    pieces, peaks, masses = (
        lax.all_to_all(
            partial_value.astype(jnp.bfloat16),
            ("seq", "sub"),
            split_axis=2,
            concat_axis=0,
            tiled=True,
        ).astype(partial_value.dtype),
        lax.all_to_all(
            peak.astype(jnp.bfloat16), ("seq", "sub"), split_axis=2, concat_axis=0, tiled=True
        ).astype(peak.dtype),
        lax.all_to_all(
            mass.astype(jnp.bfloat16), ("seq", "sub"), split_axis=2, concat_axis=0, tiled=True
        ).astype(mass.dtype),
    )
    best = jnp.max(peaks, axis=0)
    factor = jnp.exp(peaks - best[None])
    numer = jnp.sum(factor[..., None] * pieces.reshape(shards, sessions, rows, QH, HD), axis=0)
    denom = jnp.sum(factor * masses, axis=0)
    return (numer / denom[..., None]).astype(jnp.bfloat16).reshape(sessions, rows, QH * HD)


MESH = pl.DeviceIdType.MESH
CHUNKS = 4
BF = jnp.bfloat16
F32 = jnp.float32


def fused_kernel(
    shards_z,
    hid,
    wo,
    gain,
    wq,
    wkv,
    cache,
    lengths,
    cosf,
    sinf,
    out,
    hid_v,
    wo_v,
    w_v,
    k_v,
    v_v,
    p_send,
    p_recv,
    own_part,
    rs_send,
    rs_recv,
    x_all,
    acc,
    ssq,
    q_all,
    kn,
    vn,
    o_send,
    o_recv,
    fin,
    f_recv,
    in_sem,
    wo_sem,
    kvl_sem,
    kvs_sem,
    kvr_sem,
    ps_sem,
    pr_sem,
    rss_sem,
    rsr_sem,
    ags_sem,
    agr_sem,
    fws_sem,
    fwr_sem,
    qs_sem,
    qr_sem,
    os_sem,
    or_sem,
    fs_sem,
    fr_sem,
):
    Z = shards_z
    z = lax.axis_index("seq")
    c = lax.axis_index("sub")
    other = 1 - c
    rows = hid.shape[2]
    span = 2 * Z * rows
    width = wo.shape[1]
    cw = width // CHUNKS
    ql = wq.shape[1]
    heads = ql // HD
    wl = cache.shape[1]
    tile = 256
    partner = {"seq": z, "sub": other}

    def peer(d):
        return lax.rem(z + d, Z)

    def remote(src, dst, ss, rs, zz, cc):
        return pltpu.make_async_remote_copy(
            src_ref=src,
            dst_ref=dst,
            send_sem=ss,
            recv_sem=rs,
            device_id={"seq": zz, "sub": cc},
            device_id_type=MESH,
        )

    def hid_copy():
        return pltpu.make_async_copy(hid, hid_v, in_sem.at[0])

    def wo_copy(k):
        return pltpu.make_async_copy(
            wo.at[:, pl.ds(pl.multiple_of(k * cw, cw), cw)], wo_v.at[k], wo_sem.at[k]
        )

    def w_copies():
        return (
            pltpu.make_async_copy(wq, w_v.at[:, 0:ql], in_sem.at[1]),
            pltpu.make_async_copy(wkv.at[0], w_v.at[:, ql : ql + HD], in_sem.at[2]),
            pltpu.make_async_copy(wkv.at[1], w_v.at[:, ql + HD : ql + 2 * HD], in_sem.at[3]),
        )

    def kv_src(i, j, cc):
        return cache.at[i, :, pl.ds(pl.multiple_of((2 * j + cc) * HD, HD), HD)]

    def kv_dst(i, j):
        return (k_v, v_v)[i].at[j, pl.ds(pl.multiple_of(c * wl, wl), wl), :]

    def kv_local(i, j):
        return pltpu.make_async_copy(kv_src(i, j, c), kv_dst(i, j), kvl_sem.at[i, j])

    def kv_remote(i, j):
        return remote(
            kv_src(i, j, other), kv_dst(i, j), kvs_sem.at[i, j], kvr_sem.at[i, j], z, other
        )

    def pair_copy(k):
        return remote(p_send.at[k], p_recv.at[k], ps_sem.at[k], pr_sem.at[k], z, other)

    def rs_copy(k, d):
        return remote(
            rs_send.at[k, peer(d)],
            rs_recv.at[k, d],
            rss_sem.at[k, d],
            rsr_sem.at[k, d],
            peer(d),
            c,
        )

    mine = 2 * z + c

    def ag_copy(k, d):
        return remote(
            x_all.at[k, mine], x_all.at[k, mine], ags_sem.at[k, d], agr_sem.at[k, d], peer(d), c
        )

    def fw_copy(k, d):
        blk = x_all.at[k, 2 * lax.rem(z + Z - d, Z) + c]
        return remote(blk, blk, fws_sem.at[k, d], fwr_sem.at[k, d], z, other)

    def q_copy(d):
        return remote(q_all.at[z], q_all.at[z], qs_sem.at[d], qr_sem.at[d], peer(d), c)

    def o_copy(j, d):
        return remote(
            o_send.at[j, pl.ds(pl.multiple_of(peer(d) * 2 * rows, 2 * rows), 2 * rows), :],
            o_recv.at[d, j],
            os_sem.at[j, d],
            or_sem.at[j, d],
            peer(d),
            c,
        )

    def f_copy():
        src = fin.at[:, pl.ds(pl.multiple_of(other * rows, rows), rows), :]
        return remote(src, f_recv, fs_sem.at[0], fr_sem.at[0], z, other)

    hid_copy().start()
    for k in range(CHUNKS):
        wo_copy(k).start()
    barrier = pltpu.get_barrier_semaphore()
    for d in range(1, Z):
        pl.semaphore_signal(
            barrier, inc=1, device_id={"seq": peer(d), "sub": c}, device_id_type=MESH
        )
    pl.semaphore_signal(barrier, inc=1, device_id=partner, device_id_type=MESH)
    pl.semaphore_wait(barrier, Z)

    hid_copy().wait()
    ssq[...] = jnp.zeros_like(ssq)
    acc[...] = jnp.zeros_like(acc)

    def part(k, cc, store):
        lhs = hid_v[:, pl.ds(cc, 1)].reshape(Z * rows, hid.shape[3])

        def go(t, carry):
            cols = pl.ds(pl.multiple_of(t * tile, tile), tile)
            store(cols, jnp.dot(lhs, wo_v[k, :, cols], preferred_element_type=F32))
            return carry

        lax.fori_loop(0, cw // tile, go, 0)

    def pair_sum(k):
        pair_copy(k).wait_recv()
        both = own_part[k] + p_recv[k].astype(F32)
        rs_send[k] = both.astype(BF).reshape(Z, rows, cw)
        for d in range(1, Z):
            rs_copy(k, d).start()

    def stage_a(k, carry):
        wo_copy(k).wait()

        def store_p(cols, value):
            p_send[k, :, cols] = value.astype(BF)

        def store_m(cols, value):
            own_part[k, :, cols] = value

        part(k, other, store_p)
        pair_copy(k).start()
        part(k, c, store_m)

        @pl.when(k >= 1)
        def _():
            pair_sum(k - 1)

        return carry

    lax.fori_loop(0, CHUNKS, stage_a, 0)
    pair_sum(CHUNKS - 1)

    for copy in w_copies():
        copy.start()
    for i in range(2):
        for j in range(Z):
            kv_local(i, j).start()
            kv_remote(i, j).start()

    def stage_c(k, carry):
        total = rs_send[k, z].astype(F32)
        for d in range(1, Z):
            rs_copy(k, d).wait_recv()
            total = total + rs_recv[k, d].astype(F32)
        x_all[k, mine] = total.astype(BF)
        for d in range(1, Z):
            ag_copy(k, d).start()
        fw_copy(k, 0).start()
        return carry

    lax.fori_loop(0, CHUNKS, stage_c, 0)
    for copy in w_copies():
        copy.wait()

    def ag_wait(k, d):
        src = x_all.at[k, 2 * lax.rem(z + Z - d, Z) + c]
        remote(src, src, ags_sem.at[k, d], agr_sem.at[k, d], peer(d), c).wait_recv()

    def fw_wait(k, d):
        src = x_all.at[k, 2 * lax.rem(z + Z - d, Z) + other]
        remote(src, src, fws_sem.at[k, d], fwr_sem.at[k, d], z, other).wait_recv()

    def stage_d(k, carry):
        for d in range(1, Z):
            ag_wait(k, d)
            fw_copy(k, d).start()
        for d in range(Z):
            fw_wait(k, d)
        x = x_all[k].reshape(span, cw).astype(F32)
        ssq[...] += jnp.sum(x * x, axis=-1, keepdims=True)
        cols = pl.ds(pl.multiple_of(k * cw, cw), cw)
        xg = (x * gain[:, cols].astype(F32)).astype(BF)
        acc[...] += jnp.dot(xg, w_v[cols, :], preferred_element_type=F32)
        return carry

    lax.fori_loop(0, CHUNKS, stage_d, 0)

    inverse = lax.rsqrt(ssq[...] * (1.0 / width) + EPS)
    cosine = cosf[...]
    sine = sinf[...]

    def rope(value):
        return value * cosine + pltpu.roll(value, HD // 2, 1) * sine

    for h in range(heads):
        value = acc[:, h * HD : (h + 1) * HD] * inverse
        q_all[z, :, h * HD : (h + 1) * HD] = rope(value).astype(BF)
    for d in range(1, Z):
        q_copy(d).start()
    key_raw = (acc[:, ql : ql + HD] * inverse).astype(BF)
    kn[...] = rope(key_raw.astype(F32)).astype(BF)
    vn[...] = (acc[:, ql + HD : ql + 2 * HD] * inverse).astype(BF)

    for i in range(2):
        for j in range(Z):
            kv_local(i, j).wait()
            kv_remote(i, j).wait_recv()

    length = lengths[0]
    slots = z * 2 * wl + lax.broadcasted_iota(jnp.int32, (1, 2 * wl), 1)
    live = slots < length
    c2 = math.log2(math.e) / math.sqrt(HD)
    nt = (((1,), (1,)), ((), ()))
    lane = lax.broadcasted_iota(jnp.int32, (span, HD), 1)

    def attend(j, own):
        def head(h, stats):
            cols = pl.ds(pl.multiple_of(h * HD, HD), HD)
            q = q_all[j, :, cols]
            s = lax.dot_general(q, k_v[j], nt, preferred_element_type=F32)
            s = jnp.where(live, s, NEG)
            top = jnp.max(s, axis=-1, keepdims=True)
            if own:
                s2 = lax.dot_general(q, kn[...], nt, preferred_element_type=F32)
                r = lax.broadcasted_iota(jnp.int32, (span, span), 0)
                t = lax.broadcasted_iota(jnp.int32, (span, span), 1)
                s2 = jnp.where(t <= r, s2, NEG)
                top = jnp.maximum(top, jnp.max(s2, axis=-1, keepdims=True))
            top = top * c2
            p = jnp.exp2(s * c2 - top)
            total = jnp.sum(p, axis=-1, keepdims=True)
            mixed = jnp.dot(p.astype(BF), v_v[j], preferred_element_type=F32)
            if own:
                p2 = jnp.exp2(s2 * c2 - top)
                total = total + jnp.sum(p2, axis=-1, keepdims=True)
                mixed = mixed + jnp.dot(p2.astype(BF), vn[...], preferred_element_type=F32)
            o_send[j, :, cols] = (mixed * (1.0 / total)).astype(BF)
            lse = top + jnp.log2(total)
            return jnp.where((lane == h) | (lane == h + heads), lse, stats)

        stats = lax.fori_loop(0, heads, head, jnp.zeros((span, HD), F32))
        high = stats.astype(BF)
        low = (stats - high.astype(F32)).astype(BF)
        o_send[j, :, ql : ql + HD] = jnp.where(lane < heads, high.astype(F32), low.astype(F32)).astype(BF)
        for d in range(1, Z):
            o_copy(j, d).start()
        o_recv[0, j] = o_send[j, pl.ds(pl.multiple_of(z * 2 * rows, 2 * rows), 2 * rows), :]

    attend(z, True)

    def others(d, carry):
        j = lax.rem(z + Z - d, Z)
        remote(q_all.at[j], q_all.at[j], qs_sem.at[d], qr_sem.at[d], z, other).wait_recv()
        attend(j, False)
        return carry

    lax.fori_loop(1, Z, others, 0)

    def combine(j, carry):
        for d in range(1, Z):
            o_copy(j, d).wait_recv()
        stats = []
        for d in range(Z):
            both = o_recv[d, j, :, ql : ql + HD].astype(F32)
            stats.append(both + pltpu.roll(both, HD - heads, 1))
        best = functools.reduce(jnp.maximum, stats)
        shares = [jnp.exp2(s - best) for s in stats]
        inv = 1.0 / functools.reduce(lambda a, b: a + b, shares)
        shares = [s * inv for s in shares]
        for h in range(heads):
            cols = slice(h * HD, (h + 1) * HD)
            mix = None
            for d in range(Z):
                term = shares[d][:, h : h + 1] * o_recv[d, j, :, cols].astype(F32)
                mix = term if mix is None else mix + term
            fin[j, :, cols] = mix.astype(BF)
        return carry

    lax.fori_loop(0, Z, combine, 0)
    f_copy().start()
    keep = pl.ds(pl.multiple_of(c * rows, rows), rows)
    for j in range(Z):
        out[0, :, pl.ds(pl.multiple_of((2 * j + c) * ql, ql), ql)] = fin[j, keep, :]
    f_copy().wait_recv()
    for j in range(Z):
        out[0, :, pl.ds(pl.multiple_of((2 * j + other) * ql, ql), ql)] = f_recv[j]

    f_copy().wait_send()
    for i in range(2):
        for j in range(Z):
            kv_remote(i, j).wait_send()

    def drain(k, carry):
        pair_copy(k).wait_send()
        for d in range(1, Z):
            rs_copy(k, d).wait_send()
            ag_copy(k, d).wait_send()
        for d in range(Z):
            fw_copy(k, d).wait_send()
        return carry

    lax.fori_loop(0, CHUNKS, drain, 0)
    for d in range(1, Z):
        q_copy(d).wait_send()

    def drain_o(j, carry):
        for d in range(1, Z):
            o_copy(j, d).wait_send()
        return carry

    lax.fori_loop(0, Z, drain_o, 0)


def fused(gen_hidden, out_proj, norm_gain, q_weight, kv_weight, kv_cache, lengths, span_start):
    Z = lax.axis_size("seq")
    _, span, dl = gen_hidden.shape
    rows = span // (2 * Z)
    width = out_proj.shape[1]
    cw = width // CHUNKS
    ql = q_weight.shape[1]
    wl = kv_cache.shape[2]
    half = HD // 2
    freq = THETA ** (-jnp.arange(half, dtype=F32) * 2.0 / HD)
    positions = span_start[0] + jnp.arange(span, dtype=jnp.int32)
    angle = positions.astype(F32)[:, None] * freq
    cosine = jnp.cos(angle)
    sine = jnp.sin(angle)
    cosf = jnp.concatenate([cosine, cosine], axis=-1)
    sinf = jnp.concatenate([-sine, sine], axis=-1)
    any_spec = pl.BlockSpec(memory_space=pl.ANY)
    vm_spec = pl.BlockSpec(memory_space=pltpu.VMEM)
    sm_spec = pl.BlockSpec(memory_space=pltpu.SMEM)
    dma = pltpu.SemaphoreType.DMA
    V = pltpu.VMEM
    return pl.pallas_call(
        functools.partial(fused_kernel, Z),
        out_shape=jax.ShapeDtypeStruct((1, rows, 2 * Z * ql), BF),
        in_specs=[any_spec, any_spec, vm_spec, any_spec, any_spec, any_spec, sm_spec, vm_spec, vm_spec],
        out_specs=vm_spec,
        scratch_shapes=[
            V((Z, 2, rows, dl), BF),
            V((CHUNKS, dl, cw), BF),
            V((width, ql + 2 * HD), BF),
            V((Z, 2 * wl, HD), BF),
            V((Z, 2 * wl, HD), BF),
            V((CHUNKS, Z * rows, cw), BF),
            V((CHUNKS, Z * rows, cw), BF),
            V((CHUNKS, Z * rows, cw), F32),
            V((CHUNKS, Z, rows, cw), BF),
            V((CHUNKS, Z, rows, cw), BF),
            V((CHUNKS, 2 * Z, rows, cw), BF),
            V((span, ql + 2 * HD), F32),
            V((span, 1), F32),
            V((Z, span, ql), BF),
            V((span, HD), BF),
            V((span, HD), BF),
            V((Z, span, ql + HD), BF),
            V((Z, Z, 2 * rows, ql + HD), BF),
            V((Z, 2 * rows, ql), BF),
            V((Z, rows, ql), BF),
            dma((4,)),
            dma((CHUNKS,)),
            dma((2, Z)),
            dma((2, Z)),
            dma((2, Z)),
            dma((CHUNKS,)),
            dma((CHUNKS,)),
            dma((CHUNKS, Z)),
            dma((CHUNKS, Z)),
            dma((CHUNKS, Z)),
            dma((CHUNKS, Z)),
            dma((CHUNKS, Z)),
            dma((CHUNKS, Z)),
            dma((Z,)),
            dma((Z,)),
            dma((Z, Z)),
            dma((Z, Z)),
            dma((1,)),
            dma((1,)),
        ],
        compiler_params=pltpu.CompilerParams(
            collective_id=0, has_side_effects=True, vmem_limit_bytes=64000000
        ),
    )(
        gen_hidden.reshape(Z, 2, rows, dl),
        out_proj,
        norm_gain.reshape(1, width),
        q_weight,
        kv_weight,
        kv_cache.reshape(2, wl, KVH * HD),
        lengths,
        cosf,
        sinf,
    )


def solution(mesh):
    placed = (
        P(("groups", "batch"), None, ("seq", "sub")),
        P(("seq", "sub"), None),
        P(),
        P(None, ("seq", "sub")),
        P(None, None, ("seq", "sub")),
        P(None, ("groups", "batch"), ("seq", "sub"), None),
        P(("groups", "batch")),
        P(("groups", "batch")),
    )
    aligned = mesh.shape["sub"] == 2 and mesh.shape["seq"] * 2 == KVH
    return jax.shard_map(
        fused if aligned else body,
        mesh=mesh,
        in_specs=placed,
        out_specs=P(("groups", "batch"), ("seq", "sub"), None),
        check_vma=False,
    )
```

```python
import functools
import math

import jax
import jax.numpy as jnp
from jax import lax
from jax.experimental import pallas as pl
from jax.experimental.pallas import tpu as pltpu
from jax.sharding import PartitionSpec as P

QH = 32
KVH = 8
HD = 128


EPS = 1e-05
THETA = 500000.0
NEG = -1e30


def rotate(values, positions):
    half = values.shape[-1] // 2
    freq = THETA ** (-jnp.arange(half, dtype=jnp.float32) * 2.0 / values.shape[-1])
    angle = positions.astype(jnp.float32)[..., None] * freq
    cosine = jnp.cos(angle)[..., None, :]
    sine = jnp.sin(angle)[..., None, :]
    first = values[..., :half]
    second = values[..., half:]
    return jnp.concatenate(
        [first * cosine - second * sine, second * cosine + first * sine], axis=-1
    )


def body(gen_hidden, out_proj, norm_gain, q_weight, kv_weight, kv_cache, lengths, span_start):
    sessions, span, _ = gen_hidden.shape
    shards = lax.axis_size(("seq", "sub"))
    mine = lax.axis_index(("seq", "sub"))
    rows = span // shards
    local_heads = q_weight.shape[1] // HD
    group = QH // KVH
    scale = 1.0 / math.sqrt(HD)
    window_local = kv_cache.shape[2]
    summed = lax.psum(
        jnp.einsum("sci,id->csd", gen_hidden, out_proj, preferred_element_type=jnp.float32),
        ("seq", "sub"),
    )
    inputs = summed.astype(jnp.bfloat16)
    wide = inputs.astype(jnp.float32)
    inverse = lax.rsqrt(jnp.mean(wide * wide, axis=-1, keepdims=True) + EPS)
    normed = (wide * inverse * norm_gain.astype(jnp.float32)).astype(jnp.bfloat16)
    positions = span_start[None, :] + jnp.arange(span, dtype=jnp.int32)[:, None]
    query = jnp.einsum("csd,dh->csh", normed, q_weight, preferred_element_type=jnp.float32)
    query = rotate(query.reshape(span, sessions, local_heads, HD), positions).astype(jnp.bfloat16)
    kv_raw = jnp.einsum(
        "csd,jdk->jcsk", normed, kv_weight, preferred_element_type=jnp.float32
    ).astype(jnp.bfloat16)
    query_rows = jnp.arange(span, dtype=jnp.int32)
    new_rows = lax.all_to_all(kv_raw, ("seq", "sub"), split_axis=1, concat_axis=3, tiled=True)
    my_positions = lax.dynamic_slice_in_dim(positions, mine * rows, rows, 0)
    new_keys = rotate(
        new_rows[0].reshape(rows, sessions, KVH, HD).astype(jnp.float32), my_positions
    ).astype(jnp.bfloat16)
    new_values = new_rows[1].reshape(rows, sessions, KVH, HD)
    every_query = lax.all_gather(
        query.reshape(span, sessions, local_heads * HD), ("seq", "sub"), axis=2, tiled=True
    )
    grouped = every_query.reshape(span, sessions, KVH, group, HD)
    cached = kv_cache.reshape(2, sessions, window_local, KVH, HD)
    cache_scores = (
        jnp.einsum("csagh,swah->sagcw", grouped, cached[0], preferred_element_type=jnp.float32)
        * scale
    )
    slots = mine * window_local + jnp.arange(window_local, dtype=jnp.int32)
    live = slots[None, :] < lengths[:, None]
    cache_scores = jnp.where(live[:, None, None, None, :], cache_scores, NEG)
    span_scores = (
        jnp.einsum("csagh,tsah->sagct", grouped, new_keys, preferred_element_type=jnp.float32)
        * scale
    )
    key_rows = mine * rows + jnp.arange(rows, dtype=jnp.int32)
    causal = key_rows[None, :] <= query_rows[:, None]
    span_scores = jnp.where(causal, span_scores, NEG)
    top = jnp.maximum(jnp.max(cache_scores, axis=-1), jnp.max(span_scores, axis=-1))
    cache_weights = jnp.exp(cache_scores - top[..., None])
    span_weights = jnp.exp(span_scores - top[..., None])
    total = jnp.sum(cache_weights, axis=-1) + jnp.sum(span_weights, axis=-1)
    mixed = jnp.einsum(
        "sagcw,swah->scagh",
        cache_weights.astype(jnp.bfloat16),
        cached[1],
        preferred_element_type=jnp.float32,
    )
    mixed = mixed + jnp.einsum(
        "sagct,tsah->scagh",
        span_weights.astype(jnp.bfloat16),
        new_values,
        preferred_element_type=jnp.float32,
    )
    partial_value = mixed.reshape(1, sessions, span, QH * HD)
    peak = jnp.transpose(top, (0, 3, 1, 2)).reshape(1, sessions, span, QH)
    mass = jnp.transpose(total, (0, 3, 1, 2)).reshape(1, sessions, span, QH)
    pieces, peaks, masses = (
        lax.all_to_all(
            partial_value.astype(jnp.bfloat16),
            ("seq", "sub"),
            split_axis=2,
            concat_axis=0,
            tiled=True,
        ).astype(partial_value.dtype),
        lax.all_to_all(
            peak.astype(jnp.bfloat16), ("seq", "sub"), split_axis=2, concat_axis=0, tiled=True
        ).astype(peak.dtype),
        lax.all_to_all(
            mass.astype(jnp.bfloat16), ("seq", "sub"), split_axis=2, concat_axis=0, tiled=True
        ).astype(mass.dtype),
    )
    best = jnp.max(peaks, axis=0)
    factor = jnp.exp(peaks - best[None])
    numer = jnp.sum(factor[..., None] * pieces.reshape(shards, sessions, rows, QH, HD), axis=0)
    denom = jnp.sum(factor * masses, axis=0)
    return (numer / denom[..., None]).astype(jnp.bfloat16).reshape(sessions, rows, QH * HD)


MESH = pl.DeviceIdType.MESH
CHUNKS = 4
BF = jnp.bfloat16
F32 = jnp.float32


def fused_kernel(
    shards_z,
    hid,
    wo,
    gain,
    wq,
    wkv,
    cache,
    lengths,
    cosf,
    sinf,
    out,
    hid_v,
    wo_v,
    w_v,
    k_v,
    v_v,
    p_send,
    p_recv,
    own_part,
    rs_send,
    rs_recv,
    rs_merged,
    x_all,
    acc,
    ssq,
    q_all,
    kn,
    vn,
    o_send,
    o_recv,
    o_merged,
    fin,
    f_recv,
    in_sem,
    wo_sem,
    kvl_sem,
    kvs_sem,
    kvr_sem,
    ps_sem,
    pr_sem,
    rss_sem,
    rsr_sem,
    ags_sem,
    agr_sem,
    fws_sem,
    fwr_sem,
    qs_sem,
    qr_sem,
    os_sem,
    or_sem,
    fs_sem,
    fr_sem,
):
    Z = shards_z
    z = lax.axis_index("seq")
    c = lax.axis_index("sub")
    other = 1 - c
    rows = hid.shape[2]
    span = 2 * Z * rows
    width = wo.shape[1]
    cw = width // CHUNKS
    ql = wq.shape[1]
    heads = ql // HD
    wl = cache.shape[1]
    tile = 256
    partner = {"seq": z, "sub": other}

    inner = (z == 1) | (z == 2)
    near = z + 1 - 2 * lax.rem(z, 2)
    far_in = jnp.where(z < 2, 2, 1)
    far_out = jnp.where(z < 2, 3, 0)
    group_at = (z, near, far_in, far_out)
    my_in = jnp.where(z < 2, 1, 2)
    my_out = jnp.where(z < 2, 0, 3)
    merge_order = (my_out, my_in, far_in, far_out)

    def remote(src, dst, ss, rs, zz, cc):
        return pltpu.make_async_remote_copy(
            src_ref=src,
            dst_ref=dst,
            send_sem=ss,
            recv_sem=rs,
            device_id={"seq": zz, "sub": cc},
            device_id_type=MESH,
        )

    def hid_copy():
        return (
            pltpu.make_async_copy(hid.at[:, other], hid_v.at[0], in_sem.at[0]),
            pltpu.make_async_copy(hid.at[:, c], hid_v.at[1], in_sem.at[4]),
        )

    def wo_copy(k):
        return pltpu.make_async_copy(
            wo.at[:, pl.ds(pl.multiple_of(k * cw, cw), cw)], wo_v.at[k], wo_sem.at[k]
        )

    def w_copies():
        return (
            pltpu.make_async_copy(wq, w_v.at[:, 0:ql], in_sem.at[1]),
            pltpu.make_async_copy(wkv.at[0], w_v.at[:, ql : ql + HD], in_sem.at[2]),
            pltpu.make_async_copy(wkv.at[1], w_v.at[:, ql + HD : ql + 2 * HD], in_sem.at[3]),
        )

    def kv_src(i, j, cc):
        return cache.at[i, :, pl.ds(pl.multiple_of((2 * j + cc) * HD, HD), HD)]

    def kv_dst(i, j):
        return (k_v, v_v)[i].at[j, pl.ds(pl.multiple_of(c * wl, wl), wl), :]

    def kv_local(i, j):
        return pltpu.make_async_copy(kv_src(i, j, c), kv_dst(i, j), kvl_sem.at[i, j])

    def kv_remote(i, j):
        return remote(
            kv_src(i, j, other), kv_dst(i, j), kvs_sem.at[i, j], kvr_sem.at[i, j], z, other
        )

    def pair_copy(k):
        return remote(p_send.at[k], p_recv.at[k], ps_sem.at[k], pr_sem.at[k], z, other)

    mine = 2 * z + c

    def rs_copy(k, slot, who):
        return remote(
            rs_send.at[k, who],
            rs_recv.at[k, slot],
            rss_sem.at[k, slot],
            rsr_sem.at[k, slot],
            near,
            c,
        )

    def rs_cross(k, which):
        who = (far_in, far_out)[which]
        return remote(
            rs_merged.at[k, which],
            rs_recv.at[k, 4],
            rss_sem.at[k, 4 + which],
            rsr_sem.at[k, 4],
            who,
            c,
        )

    def ag_copy(k, block, slot, sem, who):
        blk = x_all.at[k, 2 * block + c]
        return remote(blk, blk, ags_sem.at[k, sem], agr_sem.at[k, slot], who, c)

    def fw_copy(k, d):
        blk = x_all.at[k, 2 * group_at[d] + c]
        return remote(blk, blk, fws_sem.at[k, d], fwr_sem.at[k, d], z, other)

    def q_copy(block, slot, sem, who):
        blk = q_all.at[block]
        return remote(blk, blk, qs_sem.at[sem], qr_sem.at[slot], who, c)

    def chip_rows(who):
        return pl.ds(pl.multiple_of(who * 2 * rows, 2 * rows), 2 * rows)

    def o_copy(j, slot, who):
        return remote(
            o_send.at[j, chip_rows(who), :],
            o_recv.at[slot, j],
            os_sem.at[j, slot],
            or_sem.at[j, slot],
            near,
            c,
        )

    def o_cross(j, which):
        who = (far_in, far_out)[which]
        return remote(
            o_merged.at[j, which],
            o_recv.at[4, j],
            os_sem.at[j, 4 + which],
            or_sem.at[j, 4],
            who,
            c,
        )

    def f_copy():
        src = fin.at[:, pl.ds(pl.multiple_of(other * rows, rows), rows), :]
        return remote(src, f_recv, fs_sem.at[0], fr_sem.at[0], z, other)

    for copy in hid_copy():
        copy.start()
    for k in range(CHUNKS):
        wo_copy(k).start()
    barrier = pltpu.get_barrier_semaphore()
    for who in (near, far_in, far_out):
        pl.semaphore_signal(
            barrier, inc=1, device_id={"seq": who, "sub": c}, device_id_type=MESH
        )
    pl.semaphore_signal(barrier, inc=1, device_id=partner, device_id_type=MESH)
    pl.semaphore_wait(barrier, Z)

    for copy in hid_copy():
        copy.wait()
    ssq[...] = jnp.zeros_like(ssq)
    acc[...] = jnp.zeros_like(acc)

    def pair_sum(k):
        pair_copy(k).wait_recv()
        both = own_part[k] + p_recv[k].astype(F32)
        rs_send[k] = both.astype(BF).reshape(Z, rows, cw)
        rs_copy(k, 1, near).start()

        @pl.when(jnp.logical_not(inner))
        def _():
            rs_copy(k, 2, far_in).start()
            rs_copy(k, 3, far_out).start()

    def stage_a(k, carry):
        wo_copy(k).wait()

        lhs = hid_v[...].reshape(span, hid.shape[3])
        half = Z * rows

        def go(t, carry):
            cols = pl.ds(pl.multiple_of(t * tile, tile), tile)
            value = jnp.dot(lhs, wo_v[k, :, cols], preferred_element_type=F32)
            p_send[k, :, cols] = value[:half].astype(BF)
            own_part[k, :, cols] = value[half:]
            return carry

        lax.fori_loop(0, cw // tile, go, 0)
        pair_copy(k).start()

        @pl.when(k >= 1)
        def _():
            pair_sum(k - 1)

        return carry

    lax.fori_loop(0, CHUNKS, stage_a, 0)
    pair_sum(CHUNKS - 1)

    for copy in w_copies():
        copy.start()
    for i in range(2):
        for j in range(Z):
            kv_local(i, j).start()
            kv_remote(i, j).start()

    def merge_rs(k):
        for which, who in ((0, far_in), (1, far_out)):
            rs_copy(k, 2 + which, who).wait_recv()
            both = rs_send[k, who].astype(F32) + rs_recv[k, 2 + which].astype(F32)
            rs_merged[k, which] = both.astype(BF)
            rs_cross(k, which).start()

    def stage_c(k):
        total = rs_send[k, z].astype(F32)
        rs_copy(k, 1, near).wait_recv()
        total = total + rs_recv[k, 1].astype(F32)
        rs_cross(k, 0).wait_recv()
        total = total + rs_recv[k, 4].astype(F32)
        x_all[k, mine] = total.astype(BF)
        ag_copy(k, z, 1, 0, near).start()

        @pl.when(inner)
        def _():
            ag_copy(k, z, 2, 1, far_in).start()

        fw_copy(k, 0).start()

    def ag_wait(k, slot):
        ag_copy(k, group_at[slot], slot, 0, near).wait_recv()

    def fw_wait(k, d):
        blk = x_all.at[k, 2 * group_at[d] + other]
        remote(blk, blk, fws_sem.at[k, d], fwr_sem.at[k, d], z, other).wait_recv()

    def stage_d(k):
        ag_wait(k, 1)
        fw_copy(k, 1).start()

        @pl.when(inner)
        def _():
            ag_copy(k, near, 3, 2, far_in).start()

        ag_wait(k, 2)
        fw_copy(k, 2).start()

        @pl.when(inner)
        def _():
            ag_copy(k, far_in, 2, 3, near).start()

        ag_wait(k, 3)
        fw_copy(k, 3).start()

        @pl.when(inner)
        def _():
            ag_copy(k, far_out, 3, 4, near).start()

    def stage_e(k):
        for d in range(Z):
            fw_wait(k, d)
        x = x_all[k].reshape(span, cw).astype(F32)
        ssq[...] += jnp.sum(x * x, axis=-1, keepdims=True)
        cols = pl.ds(pl.multiple_of(k * cw, cw), cw)
        xg = (x * gain[:, cols].astype(F32)).astype(BF)
        acc[...] += jnp.dot(xg, w_v[cols, :], preferred_element_type=F32)

    def staggered(step, carry):
        @pl.when(inner & (step < CHUNKS))
        def _():
            merge_rs(step)

        @pl.when((step >= 1) & (step < CHUNKS + 1))
        def _():
            stage_c(step - 1)

        @pl.when((step >= 2) & (step < CHUNKS + 2))
        def _():
            stage_d(step - 2)

        @pl.when(step == 3)
        def _():
            for copy in w_copies():
                copy.wait()

        @pl.when(step >= 3)
        def _():
            stage_e(step - 3)

        return carry

    lax.fori_loop(0, CHUNKS + 3, staggered, 0)

    inverse = lax.rsqrt(ssq[...] * (1.0 / width) + EPS)
    cosine = cosf[...]
    sine = sinf[...]

    def rope(value):
        return value * cosine + pltpu.roll(value, HD // 2, 1) * sine

    for h in range(heads):
        value = acc[:, h * HD : (h + 1) * HD] * inverse
        q_all[z, :, h * HD : (h + 1) * HD] = rope(value).astype(BF)
    q_copy(z, 1, 0, near).start()

    @pl.when(inner)
    def _():
        q_copy(z, 2, 1, far_in).start()

    key_raw = (acc[:, ql : ql + HD] * inverse).astype(BF)
    kn[...] = rope(key_raw.astype(F32)).astype(BF)
    vn[...] = (acc[:, ql + HD : ql + 2 * HD] * inverse).astype(BF)

    for i in range(2):
        for j in range(Z):
            kv_local(i, j).wait()
            kv_remote(i, j).wait_recv()

    length = lengths[0]
    slots = z * 2 * wl + lax.broadcasted_iota(jnp.int32, (1, 2 * wl), 1)
    live = slots < length
    c2 = math.log2(math.e) / math.sqrt(HD)
    nt = (((1,), (1,)), ((), ()))
    lane = lax.broadcasted_iota(jnp.int32, (span, HD), 1)

    def packed_stats(stats, count):
        high = stats.astype(BF).astype(F32)
        lanes = lax.broadcasted_iota(jnp.int32, (count, HD), 1)
        return jnp.where(lanes < heads, high, stats - high).astype(BF)

    def attend(j, own):
        def head(h, stats):
            cols = pl.ds(pl.multiple_of(h * HD, HD), HD)
            q = q_all[j, :, cols]
            s = lax.dot_general(q, k_v[j], nt, preferred_element_type=F32)
            s = jnp.where(live, s, NEG)
            top = jnp.max(s, axis=-1, keepdims=True)
            if own:
                s2 = lax.dot_general(q, kn[...], nt, preferred_element_type=F32)
                r = lax.broadcasted_iota(jnp.int32, (span, span), 0)
                t = lax.broadcasted_iota(jnp.int32, (span, span), 1)
                s2 = jnp.where(t <= r, s2, NEG)
                top = jnp.maximum(top, jnp.max(s2, axis=-1, keepdims=True))
            top = top * c2
            p = jnp.exp2(s * c2 - top)
            total = jnp.sum(p, axis=-1, keepdims=True)
            mixed = jnp.dot(p.astype(BF), v_v[j], preferred_element_type=F32)
            if own:
                p2 = jnp.exp2(s2 * c2 - top)
                total = total + jnp.sum(p2, axis=-1, keepdims=True)
                mixed = mixed + jnp.dot(p2.astype(BF), vn[...], preferred_element_type=F32)
            o_send[j, :, cols] = (mixed * (1.0 / total)).astype(BF)
            lse = top + jnp.log2(total)
            return jnp.where((lane == h) | (lane == h + heads), lse, stats)

        stats = lax.fori_loop(0, heads, head, jnp.zeros((span, HD), F32))
        o_send[j, :, ql : ql + HD] = packed_stats(stats, span)
        o_copy(j, 1, near).start()

        @pl.when(jnp.logical_not(inner))
        def _():
            o_copy(j, 2, far_in).start()
            o_copy(j, 3, far_out).start()

    def joined(parts):
        stats = []
        for p in parts:
            both = p[:, ql : ql + HD].astype(F32)
            stats.append(both + pltpu.roll(both, HD - heads, 1))
        best = functools.reduce(jnp.maximum, stats)
        shares = [jnp.exp2(s - best) for s in stats]
        total = functools.reduce(lambda a, b: a + b, shares)
        inv = 1.0 / total
        shares = [s * inv for s in shares]
        mixes = []
        for h in range(heads):
            cols = slice(h * HD, (h + 1) * HD)
            terms = [s[:, h : h + 1] * p[:, cols].astype(F32) for s, p in zip(shares, parts)]
            mixes.append(functools.reduce(lambda a, b: a + b, terms).astype(BF))
        return mixes, best + jnp.log2(total)

    def merge_o(j):
        for which, who in ((0, far_in), (1, far_out)):
            o_copy(j, 2 + which, who).wait_recv()
            mixes, lse = joined((o_send[j, chip_rows(who), :], o_recv[2 + which, j]))
            for h in range(heads):
                o_merged[j, which, :, h * HD : (h + 1) * HD] = mixes[h]
            low = lax.broadcasted_iota(jnp.int32, lse.shape, 1) < heads
            lse = jnp.where(low, lse, pltpu.roll(lse, heads, 1))
            o_merged[j, which, :, ql : ql + HD] = packed_stats(lse, 2 * rows)
            o_cross(j, which).start()

    attend(z, True)

    def q_wait(slot):
        q_copy(group_at[slot], slot, 0, near).wait_recv()

    q_wait(1)

    @pl.when(inner)
    def _():
        q_copy(near, 3, 2, far_in).start()

    def attend_others(slot, carry):
        j = jnp.where(slot == 1, near, jnp.where(slot == 2, far_in, far_out))

        @pl.when(slot >= 2)
        def _():
            blk = q_all.at[j]
            remote(blk, blk, qs_sem.at[0], qr_sem.at[slot], near, c).wait_recv()

            @pl.when(inner)
            def _():
                remote(blk, blk, qs_sem.at[slot + 1], qr_sem.at[slot], near, c).start()

        attend(j, False)

        @pl.when(inner)
        def _():
            merge_o(jnp.where(slot == 1, my_out, jnp.where(slot == 2, my_in, far_in)))

        return carry

    lax.fori_loop(1, Z, attend_others, 0)

    @pl.when(inner)
    def _():
        merge_o(far_out)

    def combine(j, carry):
        o_copy(j, 1, near).wait_recv()
        o_cross(j, 0).wait_recv()
        mixes, _ = joined((o_send[j, chip_rows(z), :], o_recv[1, j], o_recv[4, j]))
        for h in range(heads):
            fin[j, :, h * HD : (h + 1) * HD] = mixes[h]
        return carry

    lax.fori_loop(0, Z, combine, 0)
    f_copy().start()
    keep = pl.ds(pl.multiple_of(c * rows, rows), rows)
    for j in range(Z):
        out[0, :, pl.ds(pl.multiple_of((2 * j + c) * ql, ql), ql)] = fin[j, keep, :]
    f_copy().wait_recv()
    for j in range(Z):
        out[0, :, pl.ds(pl.multiple_of((2 * j + other) * ql, ql), ql)] = f_recv[j]

    f_copy().wait_send()
    for i in range(2):
        for j in range(Z):
            kv_remote(i, j).wait_send()

    outer = jnp.logical_not(inner)

    def drain(k, carry):
        pair_copy(k).wait_send()
        rs_copy(k, 1, near).wait_send()
        ag_copy(k, z, 1, 0, near).wait_send()
        for d in range(Z):
            fw_copy(k, d).wait_send()

        @pl.when(outer)
        def _():
            rs_copy(k, 2, far_in).wait_send()
            rs_copy(k, 3, far_out).wait_send()

        @pl.when(inner)
        def _():
            rs_cross(k, 0).wait_send()
            rs_cross(k, 1).wait_send()
            ag_copy(k, z, 2, 1, far_in).wait_send()
            ag_copy(k, near, 3, 2, far_in).wait_send()
            ag_copy(k, far_in, 2, 3, near).wait_send()
            ag_copy(k, far_out, 3, 4, near).wait_send()

        return carry

    lax.fori_loop(0, CHUNKS, drain, 0)
    q_copy(z, 1, 0, near).wait_send()

    @pl.when(inner)
    def _():
        q_copy(z, 2, 1, far_in).wait_send()
        q_copy(near, 3, 2, far_in).wait_send()
        q_copy(far_in, 2, 3, near).wait_send()
        q_copy(far_out, 3, 4, near).wait_send()

    def drain_o(j, carry):
        o_copy(j, 1, near).wait_send()

        @pl.when(outer)
        def _():
            o_copy(j, 2, far_in).wait_send()
            o_copy(j, 3, far_out).wait_send()

        @pl.when(inner)
        def _():
            o_cross(j, 0).wait_send()
            o_cross(j, 1).wait_send()

        return carry

    lax.fori_loop(0, Z, drain_o, 0)


def fused(gen_hidden, out_proj, norm_gain, q_weight, kv_weight, kv_cache, lengths, span_start):
    Z = lax.axis_size("seq")
    _, span, dl = gen_hidden.shape
    rows = span // (2 * Z)
    width = out_proj.shape[1]
    cw = width // CHUNKS
    ql = q_weight.shape[1]
    wl = kv_cache.shape[2]
    half = HD // 2
    freq = THETA ** (-jnp.arange(half, dtype=F32) * 2.0 / HD)
    positions = span_start[0] + jnp.arange(span, dtype=jnp.int32)
    angle = positions.astype(F32)[:, None] * freq
    cosine = jnp.cos(angle)
    sine = jnp.sin(angle)
    cosf = jnp.concatenate([cosine, cosine], axis=-1)
    sinf = jnp.concatenate([-sine, sine], axis=-1)
    any_spec = pl.BlockSpec(memory_space=pl.ANY)
    vm_spec = pl.BlockSpec(memory_space=pltpu.VMEM)
    sm_spec = pl.BlockSpec(memory_space=pltpu.SMEM)
    dma = pltpu.SemaphoreType.DMA
    V = pltpu.VMEM
    return pl.pallas_call(
        functools.partial(fused_kernel, Z),
        out_shape=jax.ShapeDtypeStruct((1, rows, 2 * Z * ql), BF),
        in_specs=[any_spec, any_spec, vm_spec, any_spec, any_spec, any_spec, sm_spec, vm_spec, vm_spec],
        out_specs=vm_spec,
        scratch_shapes=[
            V((2, Z, rows, dl), BF),
            V((CHUNKS, dl, cw), BF),
            V((width, ql + 2 * HD), BF),
            V((Z, 2 * wl, HD), BF),
            V((Z, 2 * wl, HD), BF),
            V((CHUNKS, Z * rows, cw), BF),
            V((CHUNKS, Z * rows, cw), BF),
            V((CHUNKS, Z * rows, cw), F32),
            V((CHUNKS, Z, rows, cw), BF),
            V((CHUNKS, Z + 1, rows, cw), BF),
            V((CHUNKS, 2, rows, cw), BF),
            V((CHUNKS, 2 * Z, rows, cw), BF),
            V((span, ql + 2 * HD), F32),
            V((span, 1), F32),
            V((Z, span, ql), BF),
            V((span, HD), BF),
            V((span, HD), BF),
            V((Z, span, ql + HD), BF),
            V((Z + 1, Z, 2 * rows, ql + HD), BF),
            V((Z, 2, 2 * rows, ql + HD), BF),
            V((Z, 2 * rows, ql), BF),
            V((Z, rows, ql), BF),
            dma((5,)),
            dma((CHUNKS,)),
            dma((2, Z)),
            dma((2, Z)),
            dma((2, Z)),
            dma((CHUNKS,)),
            dma((CHUNKS,)),
            dma((CHUNKS, 6)),
            dma((CHUNKS, 5)),
            dma((CHUNKS, 5)),
            dma((CHUNKS, Z)),
            dma((CHUNKS, Z)),
            dma((CHUNKS, Z)),
            dma((5,)),
            dma((Z,)),
            dma((Z, 6)),
            dma((Z, 5)),
            dma((1,)),
            dma((1,)),
        ],
        compiler_params=pltpu.CompilerParams(
            collective_id=0, has_side_effects=True, vmem_limit_bytes=64000000
        ),
    )(
        gen_hidden.reshape(Z, 2, rows, dl),
        out_proj,
        norm_gain.reshape(1, width),
        q_weight,
        kv_weight,
        kv_cache.reshape(2, wl, KVH * HD),
        lengths,
        cosf,
        sinf,
    )


def solution(mesh):
    placed = (
        P(("groups", "batch"), None, ("seq", "sub")),
        P(("seq", "sub"), None),
        P(),
        P(None, ("seq", "sub")),
        P(None, None, ("seq", "sub")),
        P(None, ("groups", "batch"), ("seq", "sub"), None),
        P(("groups", "batch")),
        P(("groups", "batch")),
    )
    aligned = mesh.shape["sub"] == 2 and mesh.shape["seq"] * 2 == KVH
    return jax.shard_map(
        fused if aligned else body,
        mesh=mesh,
        in_specs=placed,
        out_specs=P(("groups", "batch"), ("seq", "sub"), None),
        check_vma=False,
    )
```

```python
import functools
import math

import jax
import jax.numpy as jnp
from jax import lax
from jax.experimental import pallas as pl
from jax.experimental.pallas import tpu as pltpu
from jax.sharding import PartitionSpec as P

QH = 32
KVH = 8
HD = 128


EPS = 1e-05
THETA = 500000.0
NEG = -1e30


def rotate(values, positions):
    half = values.shape[-1] // 2
    freq = THETA ** (-jnp.arange(half, dtype=jnp.float32) * 2.0 / values.shape[-1])
    angle = positions.astype(jnp.float32)[..., None] * freq
    cosine = jnp.cos(angle)[..., None, :]
    sine = jnp.sin(angle)[..., None, :]
    first = values[..., :half]
    second = values[..., half:]
    return jnp.concatenate(
        [first * cosine - second * sine, second * cosine + first * sine], axis=-1
    )


def body(gen_hidden, out_proj, norm_gain, q_weight, kv_weight, kv_cache, lengths, span_start):
    sessions, span, _ = gen_hidden.shape
    shards = lax.axis_size(("seq", "sub"))
    mine = lax.axis_index(("seq", "sub"))
    rows = span // shards
    local_heads = q_weight.shape[1] // HD
    group = QH // KVH
    scale = 1.0 / math.sqrt(HD)
    window_local = kv_cache.shape[2]
    summed = lax.psum(
        jnp.einsum("sci,id->csd", gen_hidden, out_proj, preferred_element_type=jnp.float32),
        ("seq", "sub"),
    )
    inputs = summed.astype(jnp.bfloat16)
    wide = inputs.astype(jnp.float32)
    inverse = lax.rsqrt(jnp.mean(wide * wide, axis=-1, keepdims=True) + EPS)
    normed = (wide * inverse * norm_gain.astype(jnp.float32)).astype(jnp.bfloat16)
    positions = span_start[None, :] + jnp.arange(span, dtype=jnp.int32)[:, None]
    query = jnp.einsum("csd,dh->csh", normed, q_weight, preferred_element_type=jnp.float32)
    query = rotate(query.reshape(span, sessions, local_heads, HD), positions).astype(jnp.bfloat16)
    kv_raw = jnp.einsum(
        "csd,jdk->jcsk", normed, kv_weight, preferred_element_type=jnp.float32
    ).astype(jnp.bfloat16)
    query_rows = jnp.arange(span, dtype=jnp.int32)
    new_rows = lax.all_to_all(kv_raw, ("seq", "sub"), split_axis=1, concat_axis=3, tiled=True)
    my_positions = lax.dynamic_slice_in_dim(positions, mine * rows, rows, 0)
    new_keys = rotate(
        new_rows[0].reshape(rows, sessions, KVH, HD).astype(jnp.float32), my_positions
    ).astype(jnp.bfloat16)
    new_values = new_rows[1].reshape(rows, sessions, KVH, HD)
    every_query = lax.all_gather(
        query.reshape(span, sessions, local_heads * HD), ("seq", "sub"), axis=2, tiled=True
    )
    grouped = every_query.reshape(span, sessions, KVH, group, HD)
    cached = kv_cache.reshape(2, sessions, window_local, KVH, HD)
    cache_scores = (
        jnp.einsum("csagh,swah->sagcw", grouped, cached[0], preferred_element_type=jnp.float32)
        * scale
    )
    slots = mine * window_local + jnp.arange(window_local, dtype=jnp.int32)
    live = slots[None, :] < lengths[:, None]
    cache_scores = jnp.where(live[:, None, None, None, :], cache_scores, NEG)
    span_scores = (
        jnp.einsum("csagh,tsah->sagct", grouped, new_keys, preferred_element_type=jnp.float32)
        * scale
    )
    key_rows = mine * rows + jnp.arange(rows, dtype=jnp.int32)
    causal = key_rows[None, :] <= query_rows[:, None]
    span_scores = jnp.where(causal, span_scores, NEG)
    top = jnp.maximum(jnp.max(cache_scores, axis=-1), jnp.max(span_scores, axis=-1))
    cache_weights = jnp.exp(cache_scores - top[..., None])
    span_weights = jnp.exp(span_scores - top[..., None])
    total = jnp.sum(cache_weights, axis=-1) + jnp.sum(span_weights, axis=-1)
    mixed = jnp.einsum(
        "sagcw,swah->scagh",
        cache_weights.astype(jnp.bfloat16),
        cached[1],
        preferred_element_type=jnp.float32,
    )
    mixed = mixed + jnp.einsum(
        "sagct,tsah->scagh",
        span_weights.astype(jnp.bfloat16),
        new_values,
        preferred_element_type=jnp.float32,
    )
    partial_value = mixed.reshape(1, sessions, span, QH * HD)
    peak = jnp.transpose(top, (0, 3, 1, 2)).reshape(1, sessions, span, QH)
    mass = jnp.transpose(total, (0, 3, 1, 2)).reshape(1, sessions, span, QH)
    pieces, peaks, masses = (
        lax.all_to_all(
            partial_value.astype(jnp.bfloat16),
            ("seq", "sub"),
            split_axis=2,
            concat_axis=0,
            tiled=True,
        ).astype(partial_value.dtype),
        lax.all_to_all(
            peak.astype(jnp.bfloat16), ("seq", "sub"), split_axis=2, concat_axis=0, tiled=True
        ).astype(peak.dtype),
        lax.all_to_all(
            mass.astype(jnp.bfloat16), ("seq", "sub"), split_axis=2, concat_axis=0, tiled=True
        ).astype(mass.dtype),
    )
    best = jnp.max(peaks, axis=0)
    factor = jnp.exp(peaks - best[None])
    numer = jnp.sum(factor[..., None] * pieces.reshape(shards, sessions, rows, QH, HD), axis=0)
    denom = jnp.sum(factor * masses, axis=0)
    return (numer / denom[..., None]).astype(jnp.bfloat16).reshape(sessions, rows, QH * HD)


MESH = pl.DeviceIdType.MESH
CHUNKS = 2
BF = jnp.bfloat16
F32 = jnp.float32


def fused_kernel(
    shards_z,
    hid,
    wo,
    gain,
    wq,
    wkv,
    cache,
    lengths,
    starts,
    freqs,
    out,
    hid_v,
    wo_v,
    w_v,
    k_v,
    v_v,
    p_send,
    p_recv,
    own_part,
    rs_send,
    rs_recv,
    rs_merged,
    x_all,
    acc,
    ssq,
    q_all,
    kn,
    vn,
    o_send,
    o_recv,
    o_merged,
    fin,
    f_recv,
    rope_v,
    in_sem,
    wo_sem,
    kvl_sem,
    kvs_sem,
    kvr_sem,
    ps_sem,
    pr_sem,
    rss_sem,
    rsr_sem,
    ags_sem,
    agr_sem,
    fws_sem,
    fwr_sem,
    qs_sem,
    qr_sem,
    os_sem,
    or_sem,
    fs_sem,
    fr_sem,
):
    Z = shards_z
    z = lax.axis_index("seq")
    c = lax.axis_index("sub")
    other = 1 - c
    rows = hid.shape[2]
    span = 2 * Z * rows
    width = wo.shape[1]
    cw = width // CHUNKS
    ql = wq.shape[1]
    heads = ql // HD
    wl = cache.shape[1]
    tile = 256
    partner = {"seq": z, "sub": other}

    inner = (z == 1) | (z == 2)
    near = z + 1 - 2 * lax.rem(z, 2)
    far_in = jnp.where(z < 2, 2, 1)
    far_out = jnp.where(z < 2, 3, 0)
    group_at = (z, near, far_in, far_out)
    my_in = jnp.where(z < 2, 1, 2)
    my_out = jnp.where(z < 2, 0, 3)
    merge_order = (my_out, my_in, far_in, far_out)

    def remote(src, dst, ss, rs, zz, cc):
        return pltpu.make_async_remote_copy(
            src_ref=src,
            dst_ref=dst,
            send_sem=ss,
            recv_sem=rs,
            device_id={"seq": zz, "sub": cc},
            device_id_type=MESH,
        )

    def hid_copy():
        return (
            pltpu.make_async_copy(hid.at[:, other], hid_v.at[0], in_sem.at[0]),
            pltpu.make_async_copy(hid.at[:, c], hid_v.at[1], in_sem.at[4]),
        )

    def wo_copy(k):
        return pltpu.make_async_copy(
            wo.at[:, pl.ds(pl.multiple_of(k * cw, cw), cw)], wo_v.at[k], wo_sem.at[k]
        )

    def w_copies():
        return (
            pltpu.make_async_copy(wq, w_v.at[:, 0:ql], in_sem.at[1]),
            pltpu.make_async_copy(wkv.at[0], w_v.at[:, ql : ql + HD], in_sem.at[2]),
            pltpu.make_async_copy(wkv.at[1], w_v.at[:, ql + HD : ql + 2 * HD], in_sem.at[3]),
        )

    def kv_src(i, j, cc):
        return cache.at[i, :, pl.ds(pl.multiple_of((2 * j + cc) * HD, HD), HD)]

    def kv_dst(i, j):
        return (k_v, v_v)[i].at[j, pl.ds(pl.multiple_of(c * wl, wl), wl), :]

    def kv_local(i, j):
        return pltpu.make_async_copy(kv_src(i, j, c), kv_dst(i, j), kvl_sem.at[i, j])

    def kv_remote(i, j):
        return remote(
            kv_src(i, j, other), kv_dst(i, j), kvs_sem.at[i, j], kvr_sem.at[i, j], z, other
        )

    def pair_copy(k):
        return remote(p_send.at[k], p_recv.at[k], ps_sem.at[k], pr_sem.at[k], z, other)

    mine = 2 * z + c

    def rs_copy(k, slot, who):
        return remote(
            rs_send.at[k, who],
            rs_recv.at[k, slot],
            rss_sem.at[k, slot],
            rsr_sem.at[k, slot],
            near,
            c,
        )

    def rs_cross(k, which):
        who = (far_in, far_out)[which]
        return remote(
            rs_merged.at[k, which],
            rs_recv.at[k, 4],
            rss_sem.at[k, 4 + which],
            rsr_sem.at[k, 4],
            who,
            c,
        )

    def ag_copy(k, block, slot, sem, who):
        blk = x_all.at[k, 2 * block + c]
        return remote(blk, blk, ags_sem.at[k, sem], agr_sem.at[k, slot], who, c)

    def fw_copy(k, d):
        blk = x_all.at[k, 2 * group_at[d] + c]
        return remote(blk, blk, fws_sem.at[k, d], fwr_sem.at[k, d], z, other)

    def q_copy(block, slot, sem, who):
        blk = q_all.at[block]
        return remote(blk, blk, qs_sem.at[sem], qr_sem.at[slot], who, c)

    def chip_rows(who):
        return pl.ds(pl.multiple_of(who * 2 * rows, 2 * rows), 2 * rows)

    def o_copy(j, slot, who):
        return remote(
            o_send.at[j, chip_rows(who), :],
            o_recv.at[slot, j],
            os_sem.at[j, slot],
            or_sem.at[j, slot],
            near,
            c,
        )

    def o_cross(j, which):
        who = (far_in, far_out)[which]
        return remote(
            o_merged.at[j, which],
            o_recv.at[4, j],
            os_sem.at[j, 4 + which],
            or_sem.at[j, 4],
            who,
            c,
        )

    def f_copy():
        src = fin.at[:, pl.ds(pl.multiple_of(other * rows, rows), rows), :]
        return remote(src, f_recv, fs_sem.at[0], fr_sem.at[0], z, other)

    for copy in hid_copy():
        copy.start()
    for k in range(CHUNKS):
        wo_copy(k).start()
    barrier = pltpu.get_barrier_semaphore()
    for who in (near, far_in, far_out):
        pl.semaphore_signal(
            barrier, inc=1, device_id={"seq": who, "sub": c}, device_id_type=MESH
        )
    pl.semaphore_signal(barrier, inc=1, device_id=partner, device_id_type=MESH)
    pl.semaphore_wait(barrier, Z)

    for copy in hid_copy():
        copy.wait()
    ssq[...] = jnp.zeros_like(ssq)
    acc[...] = jnp.zeros_like(acc)

    def pair_sum(k):
        pair_copy(k).wait_recv()
        both = own_part[k] + p_recv[k].astype(F32)
        rs_send[k] = both.astype(BF).reshape(Z, rows, cw)
        rs_copy(k, 1, near).start()

        @pl.when(jnp.logical_not(inner))
        def _():
            rs_copy(k, 2, far_in).start()
            rs_copy(k, 3, far_out).start()

    def stage_a(k, carry):
        wo_copy(k).wait()

        lhs = hid_v[...].reshape(span, hid.shape[3])
        half = Z * rows

        def go(t, carry):
            cols = pl.ds(pl.multiple_of(t * tile, tile), tile)
            value = jnp.dot(lhs, wo_v[k, :, cols], preferred_element_type=F32)
            p_send[k, :, cols] = value[:half].astype(BF)
            own_part[k, :, cols] = value[half:]
            return carry

        lax.fori_loop(0, cw // tile, go, 0)
        pair_copy(k).start()

        @pl.when(k >= 1)
        def _():
            pair_sum(k - 1)

        return carry

    lax.fori_loop(0, CHUNKS, stage_a, 0)
    pair_sum(CHUNKS - 1)

    for copy in w_copies():
        copy.start()
    for i in range(2):
        for j in range(Z):
            kv_local(i, j).start()
            kv_remote(i, j).start()

    def merge_rs(k):
        for which, who in ((0, far_in), (1, far_out)):
            rs_copy(k, 2 + which, who).wait_recv()
            both = rs_send[k, who].astype(F32) + rs_recv[k, 2 + which].astype(F32)
            rs_merged[k, which] = both.astype(BF)
            rs_cross(k, which).start()

    def stage_c(k):
        total = rs_send[k, z].astype(F32)
        rs_copy(k, 1, near).wait_recv()
        total = total + rs_recv[k, 1].astype(F32)
        rs_cross(k, 0).wait_recv()
        total = total + rs_recv[k, 4].astype(F32)
        x_all[k, mine] = total.astype(BF)
        ag_copy(k, z, 1, 0, near).start()

        @pl.when(inner)
        def _():
            ag_copy(k, z, 2, 1, far_in).start()

        fw_copy(k, 0).start()

    def ag_wait(k, slot):
        ag_copy(k, group_at[slot], slot, 0, near).wait_recv()

    def fw_wait(k, d):
        blk = x_all.at[k, 2 * group_at[d] + other]
        remote(blk, blk, fws_sem.at[k, d], fwr_sem.at[k, d], z, other).wait_recv()

    def stage_d(k):
        ag_wait(k, 1)
        fw_copy(k, 1).start()

        @pl.when(inner)
        def _():
            ag_copy(k, near, 3, 2, far_in).start()

        ag_wait(k, 2)
        fw_copy(k, 2).start()

        @pl.when(inner)
        def _():
            ag_copy(k, far_in, 2, 3, near).start()

        ag_wait(k, 3)
        fw_copy(k, 3).start()

        @pl.when(inner)
        def _():
            ag_copy(k, far_out, 3, 4, near).start()

    def stage_e(k):
        for d in range(Z):
            fw_wait(k, d)
        x = x_all[k].reshape(span, cw).astype(F32)
        ssq[...] += jnp.sum(x * x, axis=-1, keepdims=True)
        cols = pl.ds(pl.multiple_of(k * cw, cw), cw)
        xg = (x * gain[cols].astype(F32).reshape(1, cw)).astype(BF)
        acc[...] += jnp.dot(xg, w_v[cols, :], preferred_element_type=F32)

    def staggered(step, carry):
        @pl.when(inner & (step < CHUNKS))
        def _():
            merge_rs(step)

        @pl.when((step >= 1) & (step < CHUNKS + 1))
        def _():
            stage_c(step - 1)

        @pl.when((step >= 2) & (step < CHUNKS + 2))
        def _():
            stage_d(step - 2)

        @pl.when(step == 3)
        def _():
            for copy in w_copies():
                copy.wait()

        @pl.when(step >= 3)
        def _():
            stage_e(step - 3)

        return carry

    angle = (starts[0] + lax.broadcasted_iota(jnp.int32, (span, HD), 0)).astype(F32) * freqs[...]
    rope_v[0] = jnp.cos(angle)
    sines = jnp.sin(angle)
    first = lax.broadcasted_iota(jnp.int32, (span, HD), 1) < HD // 2
    rope_v[1] = jnp.where(first, -sines, sines)

    lax.fori_loop(0, CHUNKS + 3, staggered, 0)

    inverse = lax.rsqrt(ssq[...] * (1.0 / width) + EPS)
    cosine = rope_v[0]
    sine = rope_v[1]

    def rope(value):
        return value * cosine + pltpu.roll(value, HD // 2, 1) * sine

    for h in range(heads):
        value = acc[:, h * HD : (h + 1) * HD] * inverse
        q_all[z, :, h * HD : (h + 1) * HD] = rope(value).astype(BF)
    q_copy(z, 1, 0, near).start()

    @pl.when(inner)
    def _():
        q_copy(z, 2, 1, far_in).start()

    key_raw = (acc[:, ql : ql + HD] * inverse).astype(BF)
    kn[...] = rope(key_raw.astype(F32)).astype(BF)
    vn[...] = (acc[:, ql + HD : ql + 2 * HD] * inverse).astype(BF)

    for i in range(2):
        for j in range(Z):
            kv_local(i, j).wait()
            kv_remote(i, j).wait_recv()

    length = lengths[0]
    slots = z * 2 * wl + lax.broadcasted_iota(jnp.int32, (1, 2 * wl), 1)
    live = slots < length
    c2 = math.log2(math.e) / math.sqrt(HD)
    nt = (((1,), (1,)), ((), ()))
    lane = lax.broadcasted_iota(jnp.int32, (span, HD), 1)

    def packed_stats(stats, count):
        high = stats.astype(BF).astype(F32)
        lanes = lax.broadcasted_iota(jnp.int32, (count, HD), 1)
        return jnp.where(lanes < heads, high, stats - high).astype(BF)

    def attend(j, own):
        def head(h, stats):
            cols = pl.ds(pl.multiple_of(h * HD, HD), HD)
            q = q_all[j, :, cols]
            s = lax.dot_general(q, k_v[j], nt, preferred_element_type=F32)
            s = jnp.where(live, s, NEG)
            top = jnp.max(s, axis=-1, keepdims=True)
            if own:
                s2 = lax.dot_general(q, kn[...], nt, preferred_element_type=F32)
                r = lax.broadcasted_iota(jnp.int32, (span, span), 0)
                t = lax.broadcasted_iota(jnp.int32, (span, span), 1)
                s2 = jnp.where(t <= r, s2, NEG)
                top = jnp.maximum(top, jnp.max(s2, axis=-1, keepdims=True))
            top = top * c2
            p = jnp.exp2(s * c2 - top)
            total = jnp.sum(p, axis=-1, keepdims=True)
            mixed = jnp.dot(p.astype(BF), v_v[j], preferred_element_type=F32)
            if own:
                p2 = jnp.exp2(s2 * c2 - top)
                total = total + jnp.sum(p2, axis=-1, keepdims=True)
                mixed = mixed + jnp.dot(p2.astype(BF), vn[...], preferred_element_type=F32)
            o_send[j, :, cols] = (mixed * (1.0 / total)).astype(BF)
            lse = top + jnp.log2(total)
            return jnp.where((lane == h) | (lane == h + heads), lse, stats)

        stats = lax.fori_loop(0, heads, head, jnp.zeros((span, HD), F32))
        o_send[j, :, ql : ql + HD] = packed_stats(stats, span)
        o_copy(j, 1, near).start()

        @pl.when(jnp.logical_not(inner))
        def _():
            o_copy(j, 2, far_in).start()
            o_copy(j, 3, far_out).start()

    def joined(parts):
        stats = []
        for p in parts:
            both = p[:, ql : ql + HD].astype(F32)
            stats.append(both + pltpu.roll(both, HD - heads, 1))
        best = functools.reduce(jnp.maximum, stats)
        shares = [jnp.exp2(s - best) for s in stats]
        total = functools.reduce(lambda a, b: a + b, shares)
        inv = 1.0 / total
        shares = [s * inv for s in shares]
        mixes = []
        for h in range(heads):
            cols = slice(h * HD, (h + 1) * HD)
            terms = [s[:, h : h + 1] * p[:, cols].astype(F32) for s, p in zip(shares, parts)]
            mixes.append(functools.reduce(lambda a, b: a + b, terms).astype(BF))
        return mixes, best + jnp.log2(total)

    def merge_o(j):
        for which, who in ((0, far_in), (1, far_out)):
            o_copy(j, 2 + which, who).wait_recv()
            mixes, lse = joined((o_send[j, chip_rows(who), :], o_recv[2 + which, j]))
            for h in range(heads):
                o_merged[j, which, :, h * HD : (h + 1) * HD] = mixes[h]
            low = lax.broadcasted_iota(jnp.int32, lse.shape, 1) < heads
            lse = jnp.where(low, lse, pltpu.roll(lse, heads, 1))
            o_merged[j, which, :, ql : ql + HD] = packed_stats(lse, 2 * rows)
            o_cross(j, which).start()

    attend(z, True)

    def q_wait(slot):
        q_copy(group_at[slot], slot, 0, near).wait_recv()

    q_wait(1)

    @pl.when(inner)
    def _():
        q_copy(near, 3, 2, far_in).start()

    def attend_others(slot, carry):
        j = jnp.where(slot == 1, near, jnp.where(slot == 2, far_in, far_out))

        @pl.when(slot >= 2)
        def _():
            blk = q_all.at[j]
            remote(blk, blk, qs_sem.at[0], qr_sem.at[slot], near, c).wait_recv()

            @pl.when(inner)
            def _():
                remote(blk, blk, qs_sem.at[slot + 1], qr_sem.at[slot], near, c).start()

        attend(j, False)

        @pl.when(inner)
        def _():
            merge_o(jnp.where(slot == 1, my_out, jnp.where(slot == 2, my_in, far_in)))

        return carry

    lax.fori_loop(1, Z, attend_others, 0)

    @pl.when(inner)
    def _():
        merge_o(far_out)

    def combine(j, carry):
        o_copy(j, 1, near).wait_recv()
        o_cross(j, 0).wait_recv()
        mixes, _ = joined((o_send[j, chip_rows(z), :], o_recv[1, j], o_recv[4, j]))
        for h in range(heads):
            fin[j, :, h * HD : (h + 1) * HD] = mixes[h]
        return carry

    lax.fori_loop(0, Z, combine, 0)
    f_copy().start()
    keep = pl.ds(pl.multiple_of(c * rows, rows), rows)
    for j in range(Z):
        out[0, :, pl.ds(pl.multiple_of((2 * j + c) * ql, ql), ql)] = fin[j, keep, :]
    f_copy().wait_recv()
    for j in range(Z):
        out[0, :, pl.ds(pl.multiple_of((2 * j + other) * ql, ql), ql)] = f_recv[j]

    f_copy().wait_send()
    for i in range(2):
        for j in range(Z):
            kv_remote(i, j).wait_send()

    outer = jnp.logical_not(inner)

    def drain(k, carry):
        pair_copy(k).wait_send()
        rs_copy(k, 1, near).wait_send()
        ag_copy(k, z, 1, 0, near).wait_send()
        for d in range(Z):
            fw_copy(k, d).wait_send()

        @pl.when(outer)
        def _():
            rs_copy(k, 2, far_in).wait_send()
            rs_copy(k, 3, far_out).wait_send()

        @pl.when(inner)
        def _():
            rs_cross(k, 0).wait_send()
            rs_cross(k, 1).wait_send()
            ag_copy(k, z, 2, 1, far_in).wait_send()
            ag_copy(k, near, 3, 2, far_in).wait_send()
            ag_copy(k, far_in, 2, 3, near).wait_send()
            ag_copy(k, far_out, 3, 4, near).wait_send()

        return carry

    lax.fori_loop(0, CHUNKS, drain, 0)
    q_copy(z, 1, 0, near).wait_send()

    @pl.when(inner)
    def _():
        q_copy(z, 2, 1, far_in).wait_send()
        q_copy(near, 3, 2, far_in).wait_send()
        q_copy(far_in, 2, 3, near).wait_send()
        q_copy(far_out, 3, 4, near).wait_send()

    def drain_o(j, carry):
        o_copy(j, 1, near).wait_send()

        @pl.when(outer)
        def _():
            o_copy(j, 2, far_in).wait_send()
            o_copy(j, 3, far_out).wait_send()

        @pl.when(inner)
        def _():
            o_cross(j, 0).wait_send()
            o_cross(j, 1).wait_send()

        return carry

    lax.fori_loop(0, Z, drain_o, 0)


def fused(gen_hidden, out_proj, norm_gain, q_weight, kv_weight, kv_cache, lengths, span_start):
    Z = lax.axis_size("seq")
    _, span, dl = gen_hidden.shape
    rows = span // (2 * Z)
    width = out_proj.shape[1]
    cw = width // CHUNKS
    ql = q_weight.shape[1]
    wl = kv_cache.shape[2]
    half = HD // 2
    freq = THETA ** (-jnp.arange(half, dtype=F32) * 2.0 / HD)
    freqs = jnp.concatenate([freq, freq])[None, :]
    any_spec = pl.BlockSpec(memory_space=pl.ANY)
    vm_spec = pl.BlockSpec(memory_space=pltpu.VMEM)
    sm_spec = pl.BlockSpec(memory_space=pltpu.SMEM)
    dma = pltpu.SemaphoreType.DMA
    V = pltpu.VMEM
    return pl.pallas_call(
        functools.partial(fused_kernel, Z),
        out_shape=jax.ShapeDtypeStruct((1, rows, 2 * Z * ql), BF),
        in_specs=[any_spec, any_spec, vm_spec, any_spec, any_spec, any_spec, sm_spec, sm_spec, vm_spec],
        out_specs=vm_spec,
        scratch_shapes=[
            V((2, Z, rows, dl), BF),
            V((CHUNKS, dl, cw), BF),
            V((width, ql + 2 * HD), BF),
            V((Z, 2 * wl, HD), BF),
            V((Z, 2 * wl, HD), BF),
            V((CHUNKS, Z * rows, cw), BF),
            V((CHUNKS, Z * rows, cw), BF),
            V((CHUNKS, Z * rows, cw), F32),
            V((CHUNKS, Z, rows, cw), BF),
            V((CHUNKS, Z + 1, rows, cw), BF),
            V((CHUNKS, 2, rows, cw), BF),
            V((CHUNKS, 2 * Z, rows, cw), BF),
            V((span, ql + 2 * HD), F32),
            V((span, 1), F32),
            V((Z, span, ql), BF),
            V((span, HD), BF),
            V((span, HD), BF),
            V((Z, span, ql + HD), BF),
            V((Z + 1, Z, 2 * rows, ql + HD), BF),
            V((Z, 2, 2 * rows, ql + HD), BF),
            V((Z, 2 * rows, ql), BF),
            V((Z, rows, ql), BF),
            V((2, span, HD), F32),
            dma((5,)),
            dma((CHUNKS,)),
            dma((2, Z)),
            dma((2, Z)),
            dma((2, Z)),
            dma((CHUNKS,)),
            dma((CHUNKS,)),
            dma((CHUNKS, 6)),
            dma((CHUNKS, 5)),
            dma((CHUNKS, 5)),
            dma((CHUNKS, Z)),
            dma((CHUNKS, Z)),
            dma((CHUNKS, Z)),
            dma((5,)),
            dma((Z,)),
            dma((Z, 6)),
            dma((Z, 5)),
            dma((1,)),
            dma((1,)),
        ],
        compiler_params=pltpu.CompilerParams(
            collective_id=0, has_side_effects=True, vmem_limit_bytes=64000000
        ),
    )(
        gen_hidden.reshape(Z, 2, rows, dl),
        out_proj,
        norm_gain,
        q_weight,
        kv_weight,
        kv_cache.reshape(2, wl, KVH * HD),
        lengths,
        span_start,
        freqs,
    )


def solution(mesh):
    placed = (
        P(("groups", "batch"), None, ("seq", "sub")),
        P(("seq", "sub"), None),
        P(),
        P(None, ("seq", "sub")),
        P(None, None, ("seq", "sub")),
        P(None, ("groups", "batch"), ("seq", "sub"), None),
        P(("groups", "batch")),
        P(("groups", "batch")),
    )
    aligned = mesh.shape["sub"] == 2 and mesh.shape["seq"] * 2 == KVH
    return jax.shard_map(
        fused if aligned else body,
        mesh=mesh,
        in_specs=placed,
        out_specs=P(("groups", "batch"), ("seq", "sub"), None),
        check_vma=False,
    )
```

```python
import functools
import math

import jax
import jax.numpy as jnp
from jax import lax
from jax.experimental import pallas as pl
from jax.experimental.pallas import tpu as pltpu
from jax.sharding import PartitionSpec as P

QH = 32
KVH = 8
HD = 128


EPS = 1e-05
THETA = 500000.0
NEG = -1e30


def rotate(values, positions):
    half = values.shape[-1] // 2
    freq = THETA ** (-jnp.arange(half, dtype=jnp.float32) * 2.0 / values.shape[-1])
    angle = positions.astype(jnp.float32)[..., None] * freq
    cosine = jnp.cos(angle)[..., None, :]
    sine = jnp.sin(angle)[..., None, :]
    first = values[..., :half]
    second = values[..., half:]
    return jnp.concatenate(
        [first * cosine - second * sine, second * cosine + first * sine], axis=-1
    )


def body(gen_hidden, out_proj, norm_gain, q_weight, kv_weight, kv_cache, lengths, span_start):
    sessions, span, _ = gen_hidden.shape
    shards = lax.axis_size(("seq", "sub"))
    mine = lax.axis_index(("seq", "sub"))
    rows = span // shards
    local_heads = q_weight.shape[1] // HD
    group = QH // KVH
    scale = 1.0 / math.sqrt(HD)
    window_local = kv_cache.shape[2]
    summed = lax.psum(
        jnp.einsum("sci,id->csd", gen_hidden, out_proj, preferred_element_type=jnp.float32),
        ("seq", "sub"),
    )
    inputs = summed.astype(jnp.bfloat16)
    wide = inputs.astype(jnp.float32)
    inverse = lax.rsqrt(jnp.mean(wide * wide, axis=-1, keepdims=True) + EPS)
    normed = (wide * inverse * norm_gain.astype(jnp.float32)).astype(jnp.bfloat16)
    positions = span_start[None, :] + jnp.arange(span, dtype=jnp.int32)[:, None]
    query = jnp.einsum("csd,dh->csh", normed, q_weight, preferred_element_type=jnp.float32)
    query = rotate(query.reshape(span, sessions, local_heads, HD), positions).astype(jnp.bfloat16)
    kv_raw = jnp.einsum(
        "csd,jdk->jcsk", normed, kv_weight, preferred_element_type=jnp.float32
    ).astype(jnp.bfloat16)
    query_rows = jnp.arange(span, dtype=jnp.int32)
    new_rows = lax.all_to_all(kv_raw, ("seq", "sub"), split_axis=1, concat_axis=3, tiled=True)
    my_positions = lax.dynamic_slice_in_dim(positions, mine * rows, rows, 0)
    new_keys = rotate(
        new_rows[0].reshape(rows, sessions, KVH, HD).astype(jnp.float32), my_positions
    ).astype(jnp.bfloat16)
    new_values = new_rows[1].reshape(rows, sessions, KVH, HD)
    every_query = lax.all_gather(
        query.reshape(span, sessions, local_heads * HD), ("seq", "sub"), axis=2, tiled=True
    )
    grouped = every_query.reshape(span, sessions, KVH, group, HD)
    cached = kv_cache.reshape(2, sessions, window_local, KVH, HD)
    cache_scores = (
        jnp.einsum("csagh,swah->sagcw", grouped, cached[0], preferred_element_type=jnp.float32)
        * scale
    )
    slots = mine * window_local + jnp.arange(window_local, dtype=jnp.int32)
    live = slots[None, :] < lengths[:, None]
    cache_scores = jnp.where(live[:, None, None, None, :], cache_scores, NEG)
    span_scores = (
        jnp.einsum("csagh,tsah->sagct", grouped, new_keys, preferred_element_type=jnp.float32)
        * scale
    )
    key_rows = mine * rows + jnp.arange(rows, dtype=jnp.int32)
    causal = key_rows[None, :] <= query_rows[:, None]
    span_scores = jnp.where(causal, span_scores, NEG)
    top = jnp.maximum(jnp.max(cache_scores, axis=-1), jnp.max(span_scores, axis=-1))
    cache_weights = jnp.exp(cache_scores - top[..., None])
    span_weights = jnp.exp(span_scores - top[..., None])
    total = jnp.sum(cache_weights, axis=-1) + jnp.sum(span_weights, axis=-1)
    mixed = jnp.einsum(
        "sagcw,swah->scagh",
        cache_weights.astype(jnp.bfloat16),
        cached[1],
        preferred_element_type=jnp.float32,
    )
    mixed = mixed + jnp.einsum(
        "sagct,tsah->scagh",
        span_weights.astype(jnp.bfloat16),
        new_values,
        preferred_element_type=jnp.float32,
    )
    partial_value = mixed.reshape(1, sessions, span, QH * HD)
    peak = jnp.transpose(top, (0, 3, 1, 2)).reshape(1, sessions, span, QH)
    mass = jnp.transpose(total, (0, 3, 1, 2)).reshape(1, sessions, span, QH)
    pieces, peaks, masses = (
        lax.all_to_all(
            partial_value.astype(jnp.bfloat16),
            ("seq", "sub"),
            split_axis=2,
            concat_axis=0,
            tiled=True,
        ).astype(partial_value.dtype),
        lax.all_to_all(
            peak.astype(jnp.bfloat16), ("seq", "sub"), split_axis=2, concat_axis=0, tiled=True
        ).astype(peak.dtype),
        lax.all_to_all(
            mass.astype(jnp.bfloat16), ("seq", "sub"), split_axis=2, concat_axis=0, tiled=True
        ).astype(mass.dtype),
    )
    best = jnp.max(peaks, axis=0)
    factor = jnp.exp(peaks - best[None])
    numer = jnp.sum(factor[..., None] * pieces.reshape(shards, sessions, rows, QH, HD), axis=0)
    denom = jnp.sum(factor * masses, axis=0)
    return (numer / denom[..., None]).astype(jnp.bfloat16).reshape(sessions, rows, QH * HD)


MESH = pl.DeviceIdType.MESH
CHUNKS = 2
BF = jnp.bfloat16
F32 = jnp.float32


def fused_kernel(
    shards_z,
    hid,
    wo,
    gain,
    wq,
    wkv,
    cache,
    lengths,
    starts,
    freqs,
    out,
    hid_v,
    wo_v,
    w_v,
    k_v,
    v_v,
    p_send,
    p_recv,
    own_part,
    rs_send,
    rs_recv,
    rs_merged,
    x_all,
    acc,
    ssq,
    q_all,
    kn,
    vn,
    o_send,
    o_recv,
    o_merged,
    fin,
    f_recv,
    rope_v,
    in_sem,
    wo_sem,
    kvl_sem,
    kvs_sem,
    kvr_sem,
    ps_sem,
    pr_sem,
    rss_sem,
    rsr_sem,
    ags_sem,
    agr_sem,
    fws_sem,
    fwr_sem,
    qs_sem,
    qr_sem,
    os_sem,
    or_sem,
    fs_sem,
    fr_sem,
):
    Z = shards_z
    z = lax.axis_index("seq")
    c = lax.axis_index("sub")
    other = 1 - c
    rows = hid.shape[2]
    span = 2 * Z * rows
    width = wo.shape[1]
    cw = width // CHUNKS
    ql = wq.shape[1]
    heads = ql // HD
    wl = cache.shape[1]
    tile = 256
    partner = {"seq": z, "sub": other}

    inner = (z == 1) | (z == 2)
    near = z + 1 - 2 * lax.rem(z, 2)
    far_in = jnp.where(z < 2, 2, 1)
    far_out = jnp.where(z < 2, 3, 0)
    group_at = (z, near, far_in, far_out)
    my_in = jnp.where(z < 2, 1, 2)
    my_out = jnp.where(z < 2, 0, 3)
    merge_order = (my_out, my_in, far_in, far_out)

    def remote(src, dst, ss, rs, zz, cc):
        return pltpu.make_async_remote_copy(
            src_ref=src,
            dst_ref=dst,
            send_sem=ss,
            recv_sem=rs,
            device_id={"seq": zz, "sub": cc},
            device_id_type=MESH,
        )

    def hid_copy():
        return (
            pltpu.make_async_copy(hid.at[:, other], hid_v.at[0], in_sem.at[0]),
            pltpu.make_async_copy(hid.at[:, c], hid_v.at[1], in_sem.at[4]),
        )

    def wo_copy(k):
        return pltpu.make_async_copy(
            wo.at[:, pl.ds(pl.multiple_of(k * cw, cw), cw)], wo_v.at[k], wo_sem.at[k]
        )

    def w_copies():
        return (
            pltpu.make_async_copy(wq, w_v.at[:, 0:ql], in_sem.at[1]),
            pltpu.make_async_copy(wkv.at[0], w_v.at[:, ql : ql + HD], in_sem.at[2]),
            pltpu.make_async_copy(wkv.at[1], w_v.at[:, ql + HD : ql + 2 * HD], in_sem.at[3]),
        )

    def kv_src(i, j, cc):
        return cache.at[i, :, pl.ds(pl.multiple_of((2 * j + cc) * HD, HD), HD)]

    def kv_dst(i, j):
        return (k_v, v_v)[i].at[j, pl.ds(pl.multiple_of(c * wl, wl), wl), :]

    def kv_local(i, j):
        return pltpu.make_async_copy(kv_src(i, j, c), kv_dst(i, j), kvl_sem.at[i, j])

    def kv_remote(i, j):
        return remote(
            kv_src(i, j, other), kv_dst(i, j), kvs_sem.at[i, j], kvr_sem.at[i, j], z, other
        )

    def pair_copy(k):
        return remote(p_send.at[k], p_recv.at[k], ps_sem.at[k], pr_sem.at[k], z, other)

    mine = 2 * z + c

    def rs_copy(k, slot, who):
        return remote(
            rs_send.at[k, who],
            rs_recv.at[k, slot],
            rss_sem.at[k, slot],
            rsr_sem.at[k, slot],
            near,
            c,
        )

    def rs_cross(k, which):
        who = (far_in, far_out)[which]
        return remote(
            rs_merged.at[k, which],
            rs_recv.at[k, 4],
            rss_sem.at[k, 4 + which],
            rsr_sem.at[k, 4],
            who,
            c,
        )

    def ag_copy(k, block, slot, sem, who):
        blk = x_all.at[k, 2 * block + c]
        return remote(blk, blk, ags_sem.at[k, sem], agr_sem.at[k, slot], who, c)

    def fw_copy(k, d):
        blk = x_all.at[k, 2 * group_at[d] + c]
        return remote(blk, blk, fws_sem.at[k, d], fwr_sem.at[k, d], z, other)

    def q_copy(block, slot, sem, who):
        blk = q_all.at[block]
        return remote(blk, blk, qs_sem.at[sem], qr_sem.at[slot], who, c)

    def chip_rows(who):
        return pl.ds(pl.multiple_of(who * 2 * rows, 2 * rows), 2 * rows)

    def o_copy(j, slot, who):
        return remote(
            o_send.at[j, chip_rows(who), :],
            o_recv.at[slot, j],
            os_sem.at[j, slot],
            or_sem.at[j, slot],
            near,
            c,
        )

    def o_cross(j, which):
        who = (far_in, far_out)[which]
        return remote(
            o_merged.at[j, which],
            o_recv.at[4, j],
            os_sem.at[j, 4 + which],
            or_sem.at[j, 4],
            who,
            c,
        )

    def f_copy():
        src = fin.at[:, pl.ds(pl.multiple_of(other * rows, rows), rows), :]
        return remote(src, f_recv, fs_sem.at[0], fr_sem.at[0], z, other)

    for copy in hid_copy():
        copy.start()
    for k in range(CHUNKS):
        wo_copy(k).start()
    barrier = pltpu.get_barrier_semaphore()
    for who in (near, far_in, far_out):
        pl.semaphore_signal(
            barrier, inc=1, device_id={"seq": who, "sub": c}, device_id_type=MESH
        )
    pl.semaphore_signal(barrier, inc=1, device_id=partner, device_id_type=MESH)
    pl.semaphore_wait(barrier, Z)

    for copy in hid_copy():
        copy.wait()
    ssq[...] = jnp.zeros_like(ssq)
    acc[...] = jnp.zeros_like(acc)

    def pair_sum(k):
        pair_copy(k).wait_recv()
        both = own_part[k] + p_recv[k].astype(F32)
        rs_send[k] = both.astype(BF).reshape(Z, rows, cw)
        @pl.when(jnp.logical_not(inner))
        def _():
            rs_copy(k, 3, far_out).start()
            rs_copy(k, 2, far_in).start()

        rs_copy(k, 1, near).start()

    def stage_a(k, carry):
        wo_copy(k).wait()

        lhs = hid_v[...].reshape(span, hid.shape[3])
        half = Z * rows

        def go(t, carry):
            cols = pl.ds(pl.multiple_of(t * tile, tile), tile)
            value = jnp.dot(lhs, wo_v[k, :, cols], preferred_element_type=F32)
            p_send[k, :, cols] = value[:half].astype(BF)
            own_part[k, :, cols] = value[half:]
            return carry

        lax.fori_loop(0, cw // tile, go, 0)
        pair_copy(k).start()

        @pl.when(k >= 1)
        def _():
            pair_sum(k - 1)

        return carry

    lax.fori_loop(0, CHUNKS, stage_a, 0)
    pair_sum(CHUNKS - 1)

    for copy in w_copies():
        copy.start()
    for i in range(2):
        for j in range(Z):
            kv_local(i, j).start()
            kv_remote(i, j).start()

    def merge_rs(k):
        for which, who in ((1, far_out), (0, far_in)):
            rs_copy(k, 2 + which, who).wait_recv()
            both = rs_send[k, who].astype(F32) + rs_recv[k, 2 + which].astype(F32)
            rs_merged[k, which] = both.astype(BF)
            rs_cross(k, which).start()

    def stage_c(k):
        total = rs_send[k, z].astype(F32)
        rs_copy(k, 1, near).wait_recv()
        total = total + rs_recv[k, 1].astype(F32)
        rs_cross(k, 0).wait_recv()
        total = total + rs_recv[k, 4].astype(F32)
        x_all[k, mine] = total.astype(BF)
        ag_copy(k, z, 1, 0, near).start()

        @pl.when(inner)
        def _():
            ag_copy(k, z, 2, 1, far_in).start()

        fw_copy(k, 0).start()

    def ag_wait(k, slot):
        ag_copy(k, group_at[slot], slot, 0, near).wait_recv()

    def fw_wait(k, d):
        blk = x_all.at[k, 2 * group_at[d] + other]
        remote(blk, blk, fws_sem.at[k, d], fwr_sem.at[k, d], z, other).wait_recv()

    def stage_d(k):
        ag_wait(k, 1)
        fw_copy(k, 1).start()

        @pl.when(inner)
        def _():
            ag_copy(k, near, 3, 2, far_in).start()

        ag_wait(k, 2)
        fw_copy(k, 2).start()

        @pl.when(inner)
        def _():
            ag_copy(k, far_in, 2, 3, near).start()

        ag_wait(k, 3)
        fw_copy(k, 3).start()

        @pl.when(inner)
        def _():
            ag_copy(k, far_out, 3, 4, near).start()

    def stage_e(k):
        for d in range(Z):
            fw_wait(k, d)
        x = x_all[k].reshape(span, cw).astype(F32)
        ssq[...] += jnp.sum(x * x, axis=-1, keepdims=True)
        cols = pl.ds(pl.multiple_of(k * cw, cw), cw)
        xg = (x * gain[cols].astype(F32).reshape(1, cw)).astype(BF)
        acc[...] += jnp.dot(xg, w_v[cols, :], preferred_element_type=F32)

    def staggered(step, carry):
        @pl.when(inner & (step < CHUNKS))
        def _():
            merge_rs(step)

        @pl.when((step >= 1) & (step < CHUNKS + 1))
        def _():
            stage_c(step - 1)

        @pl.when((step >= 2) & (step < CHUNKS + 2))
        def _():
            stage_d(step - 2)

        @pl.when(step == 3)
        def _():
            for copy in w_copies():
                copy.wait()

        @pl.when(step >= 3)
        def _():
            stage_e(step - 3)

        return carry

    angle = (starts[0] + lax.broadcasted_iota(jnp.int32, (span, HD), 0)).astype(F32) * freqs[...]
    rope_v[0] = jnp.cos(angle)
    sines = jnp.sin(angle)
    first = lax.broadcasted_iota(jnp.int32, (span, HD), 1) < HD // 2
    rope_v[1] = jnp.where(first, -sines, sines)

    lax.fori_loop(0, CHUNKS + 3, staggered, 0)

    inverse = lax.rsqrt(ssq[...] * (1.0 / width) + EPS)
    cosine = rope_v[0]
    sine = rope_v[1]

    def rope(value):
        return value * cosine + pltpu.roll(value, HD // 2, 1) * sine

    for h in range(heads):
        value = acc[:, h * HD : (h + 1) * HD] * inverse
        q_all[z, :, h * HD : (h + 1) * HD] = rope(value).astype(BF)
    q_copy(z, 1, 0, near).start()

    @pl.when(inner)
    def _():
        q_copy(z, 2, 1, far_in).start()

    key_raw = (acc[:, ql : ql + HD] * inverse).astype(BF)
    kn[...] = rope(key_raw.astype(F32)).astype(BF)
    vn[...] = (acc[:, ql + HD : ql + 2 * HD] * inverse).astype(BF)

    for i in range(2):
        for j in range(Z):
            kv_local(i, j).wait()
            kv_remote(i, j).wait_recv()

    length = lengths[0]
    slots = z * 2 * wl + lax.broadcasted_iota(jnp.int32, (1, 2 * wl), 1)
    live = slots < length
    c2 = math.log2(math.e) / math.sqrt(HD)
    nt = (((1,), (1,)), ((), ()))
    lane = lax.broadcasted_iota(jnp.int32, (span, HD), 1)

    def packed_stats(stats, count):
        high = stats.astype(BF).astype(F32)
        lanes = lax.broadcasted_iota(jnp.int32, (count, HD), 1)
        return jnp.where(lanes < heads, high, stats - high).astype(BF)

    def attend(j, own):
        def head(h, stats):
            cols = pl.ds(pl.multiple_of(h * HD, HD), HD)
            q = q_all[j, :, cols]
            s = lax.dot_general(q, k_v[j], nt, preferred_element_type=F32)
            s = jnp.where(live, s, NEG)
            top = jnp.max(s, axis=-1, keepdims=True)
            if own:
                s2 = lax.dot_general(q, kn[...], nt, preferred_element_type=F32)
                r = lax.broadcasted_iota(jnp.int32, (span, span), 0)
                t = lax.broadcasted_iota(jnp.int32, (span, span), 1)
                s2 = jnp.where(t <= r, s2, NEG)
                top = jnp.maximum(top, jnp.max(s2, axis=-1, keepdims=True))
            top = top * c2
            p = jnp.exp2(s * c2 - top)
            total = jnp.sum(p, axis=-1, keepdims=True)
            mixed = jnp.dot(p.astype(BF), v_v[j], preferred_element_type=F32)
            if own:
                p2 = jnp.exp2(s2 * c2 - top)
                total = total + jnp.sum(p2, axis=-1, keepdims=True)
                mixed = mixed + jnp.dot(p2.astype(BF), vn[...], preferred_element_type=F32)
            o_send[j, :, cols] = (mixed * (1.0 / total)).astype(BF)
            lse = top + jnp.log2(total)
            return jnp.where((lane == h) | (lane == h + heads), lse, stats)

        stats = lax.fori_loop(0, heads, head, jnp.zeros((span, HD), F32))
        o_send[j, :, ql : ql + HD] = packed_stats(stats, span)
        @pl.when(jnp.logical_not(inner))
        def _():
            o_copy(j, 3, far_out).start()
            o_copy(j, 2, far_in).start()

        o_copy(j, 1, near).start()

    def joined(parts):
        stats = []
        for p in parts:
            both = p[:, ql : ql + HD].astype(F32)
            stats.append(both + pltpu.roll(both, HD - heads, 1))
        best = functools.reduce(jnp.maximum, stats)
        shares = [jnp.exp2(s - best) for s in stats]
        total = functools.reduce(lambda a, b: a + b, shares)
        inv = 1.0 / total
        shares = [s * inv for s in shares]
        mixes = []
        for h in range(heads):
            cols = slice(h * HD, (h + 1) * HD)
            terms = [s[:, h : h + 1] * p[:, cols].astype(F32) for s, p in zip(shares, parts)]
            mixes.append(functools.reduce(lambda a, b: a + b, terms).astype(BF))
        return mixes, best + jnp.log2(total)

    def merge_o(j):
        for which, who in ((1, far_out), (0, far_in)):
            o_copy(j, 2 + which, who).wait_recv()
            mixes, lse = joined((o_send[j, chip_rows(who), :], o_recv[2 + which, j]))
            for h in range(heads):
                o_merged[j, which, :, h * HD : (h + 1) * HD] = mixes[h]
            low = lax.broadcasted_iota(jnp.int32, lse.shape, 1) < heads
            lse = jnp.where(low, lse, pltpu.roll(lse, heads, 1))
            o_merged[j, which, :, ql : ql + HD] = packed_stats(lse, 2 * rows)
            o_cross(j, which).start()

    attend(z, True)

    def q_wait(slot):
        q_copy(group_at[slot], slot, 0, near).wait_recv()

    q_wait(1)

    @pl.when(inner)
    def _():
        q_copy(near, 3, 2, far_in).start()

    def attend_others(slot, carry):
        j = jnp.where(slot == 1, near, jnp.where(slot == 2, far_in, far_out))

        @pl.when(slot >= 2)
        def _():
            blk = q_all.at[j]
            remote(blk, blk, qs_sem.at[0], qr_sem.at[slot], near, c).wait_recv()

            @pl.when(inner)
            def _():
                remote(blk, blk, qs_sem.at[slot + 1], qr_sem.at[slot], near, c).start()

        attend(j, False)

        @pl.when(inner)
        def _():
            merge_o(jnp.where(slot == 1, my_out, jnp.where(slot == 2, my_in, far_in)))

        return carry

    lax.fori_loop(1, Z, attend_others, 0)

    @pl.when(inner)
    def _():
        merge_o(far_out)

    def combine(j, carry):
        o_copy(j, 1, near).wait_recv()
        o_cross(j, 0).wait_recv()
        mixes, _ = joined((o_send[j, chip_rows(z), :], o_recv[1, j], o_recv[4, j]))
        for h in range(heads):
            fin[j, :, h * HD : (h + 1) * HD] = mixes[h]
        return carry

    lax.fori_loop(0, Z, combine, 0)
    f_copy().start()
    keep = pl.ds(pl.multiple_of(c * rows, rows), rows)
    for j in range(Z):
        out[0, :, pl.ds(pl.multiple_of((2 * j + c) * ql, ql), ql)] = fin[j, keep, :]
    f_copy().wait_recv()
    for j in range(Z):
        out[0, :, pl.ds(pl.multiple_of((2 * j + other) * ql, ql), ql)] = f_recv[j]

    f_copy().wait_send()
    for i in range(2):
        for j in range(Z):
            kv_remote(i, j).wait_send()

    outer = jnp.logical_not(inner)

    def drain(k, carry):
        pair_copy(k).wait_send()
        rs_copy(k, 1, near).wait_send()
        ag_copy(k, z, 1, 0, near).wait_send()
        for d in range(Z):
            fw_copy(k, d).wait_send()

        @pl.when(outer)
        def _():
            rs_copy(k, 2, far_in).wait_send()
            rs_copy(k, 3, far_out).wait_send()

        @pl.when(inner)
        def _():
            rs_cross(k, 0).wait_send()
            rs_cross(k, 1).wait_send()
            ag_copy(k, z, 2, 1, far_in).wait_send()
            ag_copy(k, near, 3, 2, far_in).wait_send()
            ag_copy(k, far_in, 2, 3, near).wait_send()
            ag_copy(k, far_out, 3, 4, near).wait_send()

        return carry

    lax.fori_loop(0, CHUNKS, drain, 0)
    q_copy(z, 1, 0, near).wait_send()

    @pl.when(inner)
    def _():
        q_copy(z, 2, 1, far_in).wait_send()
        q_copy(near, 3, 2, far_in).wait_send()
        q_copy(far_in, 2, 3, near).wait_send()
        q_copy(far_out, 3, 4, near).wait_send()

    def drain_o(j, carry):
        o_copy(j, 1, near).wait_send()

        @pl.when(outer)
        def _():
            o_copy(j, 2, far_in).wait_send()
            o_copy(j, 3, far_out).wait_send()

        @pl.when(inner)
        def _():
            o_cross(j, 0).wait_send()
            o_cross(j, 1).wait_send()

        return carry

    lax.fori_loop(0, Z, drain_o, 0)


def fused(gen_hidden, out_proj, norm_gain, q_weight, kv_weight, kv_cache, lengths, span_start):
    Z = lax.axis_size("seq")
    _, span, dl = gen_hidden.shape
    rows = span // (2 * Z)
    width = out_proj.shape[1]
    cw = width // CHUNKS
    ql = q_weight.shape[1]
    wl = kv_cache.shape[2]
    half = HD // 2
    freq = THETA ** (-jnp.arange(half, dtype=F32) * 2.0 / HD)
    freqs = jnp.concatenate([freq, freq])[None, :]
    any_spec = pl.BlockSpec(memory_space=pl.ANY)
    vm_spec = pl.BlockSpec(memory_space=pltpu.VMEM)
    sm_spec = pl.BlockSpec(memory_space=pltpu.SMEM)
    dma = pltpu.SemaphoreType.DMA
    V = pltpu.VMEM
    return pl.pallas_call(
        functools.partial(fused_kernel, Z),
        out_shape=jax.ShapeDtypeStruct((1, rows, 2 * Z * ql), BF),
        in_specs=[any_spec, any_spec, vm_spec, any_spec, any_spec, any_spec, sm_spec, sm_spec, vm_spec],
        out_specs=vm_spec,
        scratch_shapes=[
            V((2, Z, rows, dl), BF),
            V((CHUNKS, dl, cw), BF),
            V((width, ql + 2 * HD), BF),
            V((Z, 2 * wl, HD), BF),
            V((Z, 2 * wl, HD), BF),
            V((CHUNKS, Z * rows, cw), BF),
            V((CHUNKS, Z * rows, cw), BF),
            V((CHUNKS, Z * rows, cw), F32),
            V((CHUNKS, Z, rows, cw), BF),
            V((CHUNKS, Z + 1, rows, cw), BF),
            V((CHUNKS, 2, rows, cw), BF),
            V((CHUNKS, 2 * Z, rows, cw), BF),
            V((span, ql + 2 * HD), F32),
            V((span, 1), F32),
            V((Z, span, ql), BF),
            V((span, HD), BF),
            V((span, HD), BF),
            V((Z, span, ql + HD), BF),
            V((Z + 1, Z, 2 * rows, ql + HD), BF),
            V((Z, 2, 2 * rows, ql + HD), BF),
            V((Z, 2 * rows, ql), BF),
            V((Z, rows, ql), BF),
            V((2, span, HD), F32),
            dma((5,)),
            dma((CHUNKS,)),
            dma((2, Z)),
            dma((2, Z)),
            dma((2, Z)),
            dma((CHUNKS,)),
            dma((CHUNKS,)),
            dma((CHUNKS, 6)),
            dma((CHUNKS, 5)),
            dma((CHUNKS, 5)),
            dma((CHUNKS, Z)),
            dma((CHUNKS, Z)),
            dma((CHUNKS, Z)),
            dma((5,)),
            dma((Z,)),
            dma((Z, 6)),
            dma((Z, 5)),
            dma((1,)),
            dma((1,)),
        ],
        compiler_params=pltpu.CompilerParams(
            collective_id=0, has_side_effects=True, vmem_limit_bytes=64000000
        ),
    )(
        gen_hidden.reshape(Z, 2, rows, dl),
        out_proj,
        norm_gain,
        q_weight,
        kv_weight,
        kv_cache.reshape(2, wl, KVH * HD),
        lengths,
        span_start,
        freqs,
    )


def solution(mesh):
    placed = (
        P(("groups", "batch"), None, ("seq", "sub")),
        P(("seq", "sub"), None),
        P(),
        P(None, ("seq", "sub")),
        P(None, None, ("seq", "sub")),
        P(None, ("groups", "batch"), ("seq", "sub"), None),
        P(("groups", "batch")),
        P(("groups", "batch")),
    )
    aligned = mesh.shape["sub"] == 2 and mesh.shape["seq"] * 2 == KVH
    return jax.shard_map(
        fused if aligned else body,
        mesh=mesh,
        in_specs=placed,
        out_specs=P(("groups", "batch"), ("seq", "sub"), None),
        check_vma=False,
    )
```
